32 devices in a mesh: group: 2 (over x), expert: 16 (over z, y, core).
Axes of the slice: x: 2, y: 2, z: 4, core: 2. Of those that a mesh axis runs over, the one named last changes fastest.
Arguments:
- tokens: bfloat16 [128, 7168], P(('group', 'expert')), parts along dimension 0, may hold values from -6 to 6
- expert_ids: int32 [128, 2], P(('group', 'expert')), parts along dimension 0, may hold values from 0 to 1, all different within a row; in each aligned block of 4 rows (0 to 3, 4 to 7, ...) at most 4 rows name the same one
- gate_codes: int32 [128, 2], P(('group', 'expert')), parts along dimension 0, may hold values from 1 to 65535
- gate_weight: bfloat16 [16, 7168, 256], P('expert'), may hold values from -0.0625 to 0.0625
- up_weight: bfloat16 [16, 7168, 256], P('expert'), may hold values from -0.0625 to 0.0625
- down_weight: bfloat16 [16, 256, 7168], P('expert'), may hold values from -0.125 to 0.125
- target_basis: bfloat16 [7168, 512], P('expert'), may hold values from -0.0625 to 0.0625
Outputs:
- targets: bfloat16 [128, 512], P(('group', 'expert')), parts along dimension 0
The draws below stay inside these ranges and needn't reach their ends.
There are 2 independent parts, one for each index of `group`. The reference program is written for one: setup_inputs(seed, part) draws one part's arguments, and reference() takes and returns one part's arrays. A program takes and returns all parts, laid end to end along the dimension named above; an argument that names none is the same for every part. Nothing has to cross between parts.
Inputs may be any that keep to these rules, and one draw needn't show every extreme that they name: `expert_ids`: each row names 2 different experts; among the 4 rows of one device no expert is named more than 4 times, a bound that some block reaches.
All inputs are finite; a program needn't handle non-finite values.
Results may differ from the reference program's by a relative error of at most 0.0057.
Values may be sent and summed in bfloat16 or wider, within the bound.
No kernel may reach another device: no remote copies, remote signals or barrier semaphores. Data moves between devices by JAX's collectives and lax.ppermute only.
A program may use at most 128 MiB of HBM per device.

```python
import math
import jax
import jax.numpy as jnp
import numpy as np
from jax import lax

D = 7168
EH = 2048
R = 512
SLICES = 8
TOK_DEV = 4
EH_PART = 256
EXPERTS = 2
TOPK = 2
TOKENS = 64
CAP = 4
N_EXPERT = 16


def place_ends(drawn, rng, least, largest):
    longest = drawn.shape.index(max(drawn.shape))
    spots = []
    for shift in (0, 1):
        where = [jax.random.randint(jax.random.fold_in(rng, axis), (), 0, length) for axis, length in enumerate(drawn.shape)]
        where[longest] = (where[longest] + shift) % drawn.shape[longest]
        spots.append(tuple(where))
    return drawn.at[spots[0]].set(least).at[spots[1]].set(largest)


def block_levels(rng, dims, cuts, least, top_value):
    gain = 1.0
    for position, blocks in cuts:
        heights = jax.random.uniform(jax.random.fold_in(jax.random.fold_in(rng, 6), position), (blocks,), jnp.float32, least / len(cuts), top_value / len(cuts))
        gain = gain * jnp.repeat(jnp.exp(heights), dims[position] // blocks).reshape((-1,) + (1,) * (len(dims) - 1 - position))
    return gain


def routed_block(key, own, number, rows, amount, top, bound, lean):
    ranking = jax.random.permutation(key, amount)
    crowded, usual = load_shares(amount, rows * top, bound, lean, True), load_shares(amount, rows * top, bound, lean, False)
    places = jnp.arange(amount)

    def named(sizes, rotation):
        used = int((sizes > 0).sum())
        fixed = max(1, used // 4)
        passed = fixed + (places - fixed + rotation * (used - fixed)) % max(1, amount - fixed)
        return jnp.zeros((amount,), jnp.int32).at[ranking[jnp.where(places < fixed, places, passed)]].set(jnp.asarray(sizes, jnp.int32))

    sizes = jnp.where(number % 4 == 0, named(crowded, number // 4), named(usual, number - number // 4 - 1))
    mixed = jax.random.permutation(jax.random.fold_in(own, 3), amount)
    donor, receiver = mixed[0:amount // 2 * 2:2], mixed[1:amount // 2 * 2:2]
    slack = jnp.minimum(sizes[donor] - 1, bound - sizes[receiver]) // 2
    slack = jnp.where((donor == ranking[0]) | (receiver == ranking[0]) | (sizes[receiver] == 0), 0, jnp.maximum(slack, 0))
    passed = jax.random.randint(jax.random.fold_in(own, 4), (amount // 2,), 0, 1 << 20) % (slack + 1)
    sizes = sizes.at[donor].add(-passed).at[receiver].add(passed)
    labels = jnp.searchsorted(jnp.cumsum(sizes), jnp.arange(rows * top), side="right").astype(jnp.int32)
    table = labels.reshape(top, rows).T
    table = table[jax.random.permutation(jax.random.fold_in(own, 1), rows)]
    rotation = jax.random.randint(jax.random.fold_in(own, 2), (rows, 1), 0, top)
    return jnp.take_along_axis(table, (jnp.arange(top)[None, :] + rotation) % top, axis=1)


def load_shares(count, total, limit, slope, full):
    portions = [(1 << 20) // math.isqrt(rank ** slope) + 1 for rank in range(1, count + 1)]
    largest = limit if full else min(limit, max(-(-total // count), total * portions[0] // sum(portions)))
    least = 1 if total - largest >= count - 1 else 0
    given, rest = [largest] + [least] * (count - 1), total - largest - least * (count - 1)
    while rest > 0:
        free = [i for i in range(1, count) if given[i] < largest] or [i for i in range(1, count) if given[i] < limit]
        whole, remaining = sum([portions[i] for i in free]), rest
        for i in free:
            more = min(limit - given[i], max(1, remaining * portions[i] // whole), rest)
            given[i] = given[i] + more
            rest = rest - more
    return np.array(given)


def centred(stream_key, shape, width, bound, pieces=(), kind=jnp.bfloat16):
    factor_of = block_levels(stream_key, shape, pieces, -0.22, 0.18) if pieces else 1.0
    values = jax.random.normal(stream_key, shape, jnp.float32) * width * factor_of
    return jnp.minimum(jnp.maximum(values, -bound), bound).astype(kind)


def setup_inputs(seed: int = 0, part: int = 0) -> dict:
    keys = jax.random.split(jax.random.key(seed), 8)
    part_splits = jax.random.split(jax.random.fold_in(keys[7], part), 8)
    tokens = centred(part_splits[0], (TOKENS, D), 1.0, 6.0, ((0, 16),))
    expert_ids_keys = jax.random.split(jax.random.fold_in(part_splits[1], 1), TOKENS // TOK_DEV)
    expert_ids_turns = jax.random.permutation(jax.random.fold_in(part_splits[1], 3), TOKENS // TOK_DEV)
    expert_ids = jax.vmap(lambda own, number: routed_block(jax.random.fold_in(part_splits[1], 2), own, number, TOK_DEV, EXPERTS, TOPK, CAP, 2))(expert_ids_keys, expert_ids_turns).reshape((TOKENS, TOPK))
    gate_codes = place_ends(jax.random.randint(part_splits[2], (TOKENS, TOPK), 1, 65536), jax.random.fold_in(part_splits[2], 1), 1, 65535).astype(jnp.int32)
    gate_weight = centred(keys[3], (N_EXPERT, D, EH_PART), D ** -0.5, 0.0625, ((0, 16),))
    up_weight = centred(keys[4], (N_EXPERT, D, EH_PART), D ** -0.5, 0.0625, ((0, 16),))
    down_weight = centred(keys[5], (N_EXPERT, EH_PART, D), EH ** -0.5, 0.125, ((0, 16),))
    target_basis = centred(keys[6], (D, R), D ** -0.5, 0.0625, ((0, 16),))
    return dict(tokens=tokens, expert_ids=expert_ids, gate_codes=gate_codes, gate_weight=gate_weight, up_weight=up_weight, down_weight=down_weight, target_basis=target_basis)


def reference(tokens, expert_ids, gate_codes, gate_weight, up_weight, down_weight, target_basis):
    flat_ids = expert_ids.reshape(-1)
    onehot = (flat_ids[:, None] == jnp.arange(EXPERTS, dtype=jnp.int32)[None, :]).astype(jnp.int32)
    before = jnp.cumsum(onehot, axis=0) - onehot
    slot_rank = jnp.sum(before * onehot, axis=1).astype(jnp.int32)
    row_token = (jnp.arange(TOKENS * TOPK, dtype=jnp.int32) // TOPK).astype(jnp.int32)
    slot_table = jnp.full((EXPERTS, N_EXPERT * CAP), TOKENS, jnp.int32).at[flat_ids, slot_rank].set(row_token)
    padded = jnp.concatenate([tokens, jnp.zeros((1, D), tokens.dtype)], axis=0)
    gate_split = gate_weight.reshape(EXPERTS, SLICES, D, EH_PART)
    up_split = up_weight.reshape(EXPERTS, SLICES, D, EH_PART)
    down_split = down_weight.reshape(EXPERTS, SLICES, EH_PART, D)

    def expert_work(inputs):
        expert_table, gate_mats, up_mats, down_mats = inputs
        row_block = padded[expert_table]
        total = jnp.zeros((N_EXPERT * CAP, R), jnp.float32)
        for slice_index in range(SLICES):
            gate_act = jnp.dot(row_block, gate_mats[slice_index], preferred_element_type=jnp.float32)
            up_act = jnp.dot(row_block, up_mats[slice_index], preferred_element_type=jnp.float32)
            hidden = (jax.nn.silu(gate_act) * up_act).astype(jnp.bfloat16)
            expert_part = jnp.dot(hidden, down_mats[slice_index], preferred_element_type=jnp.float32).astype(jnp.bfloat16)
            total = total + jnp.dot(expert_part, target_basis, preferred_element_type=jnp.float32)
        return total

    per_expert = lax.map(expert_work, (slot_table, gate_split, up_split, down_split))
    projected = per_expert[expert_ids, slot_rank.reshape(TOKENS, TOPK)]
    codes_float = gate_codes.astype(jnp.float32)
    weights = 2.5 * codes_float / jnp.sum(codes_float, axis=1, keepdims=True)
    return jnp.sum(weights[:, :, None] * projected, axis=1).astype(jnp.bfloat16)
```

```python
import functools

import jax
import jax.numpy as jnp
from jax import lax
from jax.experimental import pallas as pl
from jax.experimental.pallas import tpu as pltpu
from jax.sharding import PartitionSpec as P

SLICES = 8
CORES = 2
LANES = 128
MIB = 1 << 20


def run_expert(received, gate_weight, up_weight, down_weight):
    sources, slots, feature_width = received.shape
    row_block = received.reshape(sources * slots, feature_width)
    gate_act = jnp.dot(row_block, gate_weight[0], preferred_element_type=jnp.float32)
    up_act = jnp.dot(row_block, up_weight[0], preferred_element_type=jnp.float32)
    hidden = (jax.nn.silu(gate_act) * up_act).astype(jnp.bfloat16)
    expert_part = jnp.dot(hidden, down_weight[0], preferred_element_type=jnp.float32).astype(
        jnp.bfloat16
    )
    return expert_part.reshape(sources, slots, feature_width)


def general_shards(
    tokens, expert_ids, gate_codes, gate_weight, up_weight, down_weight, target_basis
):
    token_count, feature_width = tokens.shape
    pick_count = expert_ids.shape[1]
    owner_count = lax.axis_size("expert")
    expert_count = owner_count // SLICES
    capacity = min(token_count, max(2, 5 * token_count * pick_count // (4 * expert_count)))
    rank_width = target_basis.shape[1]
    flat_ids = expert_ids.reshape(-1)
    onehot = (flat_ids[:, None] == jnp.arange(expert_count, dtype=jnp.int32)[None, :]).astype(
        jnp.int32
    )
    before = jnp.cumsum(onehot, axis=0) - onehot
    slot_rank = jnp.sum(before * onehot, axis=1)
    slot_index = flat_ids * capacity + slot_rank
    row_token = jnp.arange(token_count * pick_count, dtype=jnp.int32) // pick_count
    slot_table = (
        jnp.full((expert_count * capacity,), token_count, jnp.int32).at[slot_index].set(row_token)
    )
    padded = jnp.concatenate([tokens, jnp.zeros((1, feature_width), tokens.dtype)], axis=0)
    per_expert_rows = padded[slot_table].reshape(expert_count, 1, capacity, feature_width)
    outgoing = jnp.broadcast_to(per_expert_rows, (expert_count, SLICES, capacity, feature_width))
    outgoing = outgoing.reshape(owner_count, capacity, feature_width)
    full_basis = lax.all_gather(target_basis, "expert", axis=0, tiled=True)
    expert_part = run_expert(
        lax.all_to_all(outgoing, "expert", split_axis=0, concat_axis=0, tiled=True),
        gate_weight,
        up_weight,
        down_weight,
    )
    result = jnp.einsum("skd,dr->skr", expert_part, full_basis, preferred_element_type=jnp.float32)
    returned = lax.all_to_all(result, "expert", split_axis=0, concat_axis=0, tiled=True)
    summed = jnp.sum(returned.reshape(expert_count, SLICES, capacity, rank_width), axis=1)
    projected = summed.reshape(expert_count * capacity, rank_width)[slot_index]
    codes_float = gate_codes.astype(jnp.float32)
    weights = 2.5 * codes_float / jnp.sum(codes_float, axis=1, keepdims=True)
    projected = projected.reshape(token_count, pick_count, rank_width)
    return jnp.sum(weights[:, :, None] * projected, axis=1).astype(jnp.bfloat16)


def expert_kernel(chips, me_ref, *refs):
    blocks = refs[: 2 * chips]
    gate_hbm, up_hbm, down_hbm, mine_ref, other_ref, x_ref, gate_v, up_v, down_v, sems = refs[
        2 * chips :
    ]
    rows, width = blocks[0].shape
    half = chips * rows
    hidden_units = gate_v.shape[1]
    span = width // chips
    copies = []
    for k in range(chips):
        part = pl.ds(k * span, span)
        copies.append(
            (
                pltpu.make_async_copy(gate_hbm.at[0, part, :], gate_v.at[part, :], sems.at[0, k]),
                pltpu.make_async_copy(up_hbm.at[0, part, :], up_v.at[part, :], sems.at[1, k]),
            )
        )
    for gate_copy, up_copy in copies:
        gate_copy.start()
        up_copy.start()
    down_copies = []
    for k in range(chips):
        part = pl.ds(k * span, span)
        down_copies.append(
            pltpu.make_async_copy(down_hbm.at[0, :, part], down_v.at[:, part], sems.at[2, k])
        )
        down_copies[k].start()
    for b, block in enumerate(blocks):
        x_ref[b * rows : (b + 1) * rows, :] = block[...]
    gate_act = jnp.zeros((2 * half, hidden_units), jnp.float32)
    up_act = jnp.zeros((2 * half, hidden_units), jnp.float32)
    for k, (gate_copy, up_copy) in enumerate(copies):
        part = slice(k * span, (k + 1) * span)
        x_part = x_ref[:, part]
        gate_copy.wait()
        gate_act += jnp.dot(x_part, gate_v[part, :], preferred_element_type=jnp.float32)
        up_copy.wait()
        up_act += jnp.dot(x_part, up_v[part, :], preferred_element_type=jnp.float32)
    hidden = (gate_act / (1.0 + jnp.exp(-gate_act)) * up_act).astype(jnp.bfloat16)
    to_row = lax.broadcasted_iota(jnp.int32, (2 * half, 2 * half), 0)
    from_row = lax.broadcasted_iota(jnp.int32, (2 * half, 2 * half), 1)
    wanted = jnp.bitwise_xor(from_row, me_ref[0] * rows)
    order = jnp.where(to_row == wanted, 1.0, 0.0).astype(jnp.bfloat16)
    hidden = jnp.dot(order, hidden, preferred_element_type=jnp.float32).astype(jnp.bfloat16)
    for k in range(chips):
        part = slice(k * span, (k + 1) * span)
        down_copies[k].wait()
        out = jnp.dot(hidden, down_v[:, part], preferred_element_type=jnp.float32)
        out = out.astype(jnp.bfloat16)
        mine_ref[k] = out[:half]
        other_ref[k] = out[half:]


def basis_kernel(experts, core_ref, parts_ref, mine_ref, other_ref, out_ref, basis_ref):
    chips, half, span = parts_ref.shape
    shard = mine_ref.shape[0]
    core = core_ref[0]
    basis_ref[pl.ds(pl.multiple_of(core * shard, shard), shard), :] = mine_ref[...]
    basis_ref[pl.ds(pl.multiple_of((1 - core) * shard, shard), shard), :] = other_ref[...]
    per = chips // experts
    rows = half // chips
    high, low = [], []
    for e in range(experts):
        total = parts_ref[e * per].astype(jnp.float32)
        for s in range(1, per):
            total += parts_ref[e * per + s].astype(jnp.float32)
        top = total.astype(jnp.bfloat16)
        high.append(top)
        low.append((total - top.astype(jnp.float32)).astype(jnp.bfloat16))
    stacked = jnp.concatenate(high + low, axis=0)
    out = jnp.dot(stacked, basis_ref[...], preferred_element_type=jnp.float32)
    out = out[: experts * half] + out[experts * half :]
    for e in range(experts):
        for j in range(chips):
            at = e * half + j * rows
            out_ref[j, e * rows : (e + 1) * rows, :] = out[at : at + rows].astype(out_ref.dtype)


def sharded_basis_shards(
    tokens, expert_ids, gate_codes, gate_weight, up_weight, down_weight, target_basis
):
    rows, width = tokens.shape
    devices = lax.axis_size("expert")
    chips = devices // CORES
    experts = devices // SLICES
    half = chips * rows
    span = width // chips
    hidden_units = gate_weight.shape[2]
    shard, rank = target_basis.shape
    index = lax.axis_index("expert").astype(jnp.int32)
    chip = (index // CORES).reshape(1)
    core = (index % CORES).reshape(1)
    groups = [list(range(c, devices, CORES)) for c in range(CORES)]

    def swap(x, step):
        return lax.ppermute(x, "expert", [(i, i ^ step) for i in range(devices)])

    mine = [tokens] + [swap(tokens, CORES * d) for d in range(1, chips)]
    other = [swap(block, 1) for block in mine]
    other_basis = swap(target_basis, 1)

    vmem = pl.BlockSpec(memory_space=pltpu.VMEM)
    smem = pl.BlockSpec(memory_space=pltpu.SMEM)
    hbm = pl.BlockSpec(memory_space=pl.ANY)
    part_shape = jax.ShapeDtypeStruct((chips, half, span), jnp.bfloat16)
    mine_part, other_part = pl.pallas_call(
        functools.partial(expert_kernel, chips),
        out_shape=(part_shape, part_shape),
        in_specs=[smem] + [vmem] * (2 * chips) + [hbm] * 3,
        out_specs=(vmem, vmem),
        scratch_shapes=[
            pltpu.VMEM((2 * half, width), jnp.bfloat16),
            pltpu.VMEM((width, hidden_units), jnp.bfloat16),
            pltpu.VMEM((width, hidden_units), jnp.bfloat16),
            pltpu.VMEM((hidden_units, width), jnp.bfloat16),
            pltpu.SemaphoreType.DMA((3, chips)),
        ],
        compiler_params=pltpu.CompilerParams(vmem_limit_bytes=24 * MIB),
        name="expert_work",
    )(chip, *mine, *other, gate_weight, up_weight, down_weight)
    from_core = swap(other_part, 1)
    pair_part = (mine_part.astype(jnp.float32) + from_core.astype(jnp.float32)).astype(jnp.bfloat16)
    parts = lax.all_to_all(
        pair_part, "expert", split_axis=0, concat_axis=0, axis_index_groups=groups
    )
    partial = pl.pallas_call(
        functools.partial(basis_kernel, experts),
        out_shape=jax.ShapeDtypeStruct((chips, experts * rows, rank), jnp.float32),
        in_specs=[smem, vmem, vmem, vmem],
        out_specs=vmem,
        scratch_shapes=[pltpu.VMEM((CORES * shard, rank), jnp.bfloat16)],
        compiler_params=pltpu.CompilerParams(vmem_limit_bytes=16 * MIB),
        name="basis_product",
    )(core, parts, target_basis, other_basis)
    returned = lax.all_to_all(
        partial, "expert", split_axis=0, concat_axis=0, axis_index_groups=groups
    )
    projected = jnp.sum(returned, axis=0).reshape(experts, rows, rank)
    codes_float = gate_codes.astype(jnp.float32)
    weights = 2.5 * codes_float / jnp.sum(codes_float, axis=1, keepdims=True)
    chosen = expert_ids[None, :, :] == jnp.arange(experts, dtype=jnp.int32)[:, None, None]
    per_expert = jnp.sum(jnp.where(chosen, weights[None, :, :], 0.0), axis=2)
    return jnp.sum(per_expert[:, :, None] * projected, axis=0).astype(jnp.bfloat16)


def fits(tokens, target_basis):
    rows, width = tokens.shape
    devices = lax.axis_size("expert")
    chips = devices // CORES
    return (
        devices % (CORES * SLICES) == 0
        and chips & (chips - 1) == 0
        and chips <= SLICES
        and rows & (rows - 1) == 0
        and width % (chips * LANES) == 0
        and target_basis.shape[0] * CORES * chips == width
        and target_basis.shape[0] % 16 == 0
    )


def shards(tokens, expert_ids, gate_codes, gate_weight, up_weight, down_weight, target_basis):
    plan = sharded_basis_shards if fits(tokens, target_basis) else general_shards
    return plan(
        tokens, expert_ids, gate_codes, gate_weight, up_weight, down_weight, target_basis
    )


def solution(mesh):
    in_specs = (
        P(("group", "expert"), None),
        P(("group", "expert"), None),
        P(("group", "expert"), None),
        P("expert", None, None),
        P("expert", None, None),
        P("expert", None, None),
        P("expert", None),
    )
    out_specs = P(("group", "expert"), None)
    return jax.shard_map(shards, mesh=mesh, in_specs=in_specs, out_specs=out_specs, check_vma=False)
```

```python
import functools

import jax
import jax.numpy as jnp
from jax import lax
from jax.experimental import pallas as pl
from jax.experimental.pallas import tpu as pltpu
from jax.sharding import PartitionSpec as P

SLICES = 8
CORES = 2
LANES = 128
MIB = 1 << 20


def run_expert(received, gate_weight, up_weight, down_weight):
    sources, slots, feature_width = received.shape
    row_block = received.reshape(sources * slots, feature_width)
    gate_act = jnp.dot(row_block, gate_weight[0], preferred_element_type=jnp.float32)
    up_act = jnp.dot(row_block, up_weight[0], preferred_element_type=jnp.float32)
    hidden = (jax.nn.silu(gate_act) * up_act).astype(jnp.bfloat16)
    expert_part = jnp.dot(hidden, down_weight[0], preferred_element_type=jnp.float32).astype(
        jnp.bfloat16
    )
    return expert_part.reshape(sources, slots, feature_width)


def general_shards(
    tokens, expert_ids, gate_codes, gate_weight, up_weight, down_weight, target_basis
):
    token_count, feature_width = tokens.shape
    pick_count = expert_ids.shape[1]
    owner_count = lax.axis_size("expert")
    expert_count = owner_count // SLICES
    capacity = min(token_count, max(2, 5 * token_count * pick_count // (4 * expert_count)))
    rank_width = target_basis.shape[1]
    flat_ids = expert_ids.reshape(-1)
    onehot = (flat_ids[:, None] == jnp.arange(expert_count, dtype=jnp.int32)[None, :]).astype(
        jnp.int32
    )
    before = jnp.cumsum(onehot, axis=0) - onehot
    slot_rank = jnp.sum(before * onehot, axis=1)
    slot_index = flat_ids * capacity + slot_rank
    row_token = jnp.arange(token_count * pick_count, dtype=jnp.int32) // pick_count
    slot_table = (
        jnp.full((expert_count * capacity,), token_count, jnp.int32).at[slot_index].set(row_token)
    )
    padded = jnp.concatenate([tokens, jnp.zeros((1, feature_width), tokens.dtype)], axis=0)
    per_expert_rows = padded[slot_table].reshape(expert_count, 1, capacity, feature_width)
    outgoing = jnp.broadcast_to(per_expert_rows, (expert_count, SLICES, capacity, feature_width))
    outgoing = outgoing.reshape(owner_count, capacity, feature_width)
    full_basis = lax.all_gather(target_basis, "expert", axis=0, tiled=True)
    expert_part = run_expert(
        lax.all_to_all(outgoing, "expert", split_axis=0, concat_axis=0, tiled=True),
        gate_weight,
        up_weight,
        down_weight,
    )
    result = jnp.einsum("skd,dr->skr", expert_part, full_basis, preferred_element_type=jnp.float32)
    returned = lax.all_to_all(result, "expert", split_axis=0, concat_axis=0, tiled=True)
    summed = jnp.sum(returned.reshape(expert_count, SLICES, capacity, rank_width), axis=1)
    projected = summed.reshape(expert_count * capacity, rank_width)[slot_index]
    codes_float = gate_codes.astype(jnp.float32)
    weights = 2.5 * codes_float / jnp.sum(codes_float, axis=1, keepdims=True)
    projected = projected.reshape(token_count, pick_count, rank_width)
    return jnp.sum(weights[:, :, None] * projected, axis=1).astype(jnp.bfloat16)


def fetch_kernel(chips, *refs):
    sources, targets, sems = refs[:3], refs[3:6], refs[6]
    copies = []
    for w in range(3):
        rows = sources[w].shape[1] // chips
        for k in range(chips):
            part = pl.ds(k * rows, rows)
            copy = pltpu.make_async_copy(
                sources[w].at[0, part, :], targets[w].at[part, :], sems.at[w, k]
            )
            copy.start()
            copies.append(copy)
    for copy in copies:
        copy.wait()


def expert_kernel(order, me_ref, *refs):
    chips = len(order)
    blocks = refs[: 2 * chips]
    gate_ref, up_ref, down_ref, mine_ref, other_ref, x_ref = refs[2 * chips :]
    rows, width = blocks[0].shape
    half = chips * rows
    span = width // chips
    for b, block in enumerate(blocks):
        at = b // chips * half + order[b % chips] * rows
        x_ref[at : at + rows, :] = block[...]
    x = x_ref[...]
    gate_act = jnp.dot(x, gate_ref[...], preferred_element_type=jnp.float32)
    up_act = jnp.dot(x, up_ref[...], preferred_element_type=jnp.float32)
    hidden = (gate_act / (1.0 + jnp.exp(-gate_act)) * up_act).astype(jnp.bfloat16)
    to_row = lax.broadcasted_iota(jnp.int32, (2 * half, 2 * half), 0)
    from_row = lax.broadcasted_iota(jnp.int32, (2 * half, 2 * half), 1)
    wanted = jnp.bitwise_xor(from_row, me_ref[0] * rows)
    chip_order = jnp.where(to_row == wanted, 1.0, 0.0).astype(jnp.bfloat16)
    hidden = jnp.dot(chip_order, hidden, preferred_element_type=jnp.float32).astype(jnp.bfloat16)
    for k in range(chips):
        part = slice(k * span, (k + 1) * span)
        out = jnp.dot(hidden, down_ref[:, part], preferred_element_type=jnp.float32)
        out = out.astype(jnp.bfloat16)
        mine_ref[k] = out[:half]
        other_ref[k] = out[half:]


def basis_kernel(experts, core_ref, parts_ref, mine_ref, other_ref, out_ref, basis_ref):
    chips, half, span = parts_ref.shape
    shard = mine_ref.shape[0]
    core = core_ref[0]
    basis_ref[pl.ds(pl.multiple_of(core * shard, shard), shard), :] = mine_ref[...]
    basis_ref[pl.ds(pl.multiple_of((1 - core) * shard, shard), shard), :] = other_ref[...]
    per = chips // experts
    rows = half // chips
    high, low = [], []
    for e in range(experts):
        total = parts_ref[e * per].astype(jnp.float32)
        for s in range(1, per):
            total += parts_ref[e * per + s].astype(jnp.float32)
        top = total.astype(jnp.bfloat16)
        high.append(top)
        low.append((total - top.astype(jnp.float32)).astype(jnp.bfloat16))
    stacked = jnp.concatenate(high + low, axis=0)
    out = jnp.dot(stacked, basis_ref[...], preferred_element_type=jnp.float32)
    out = out[: experts * half] + out[experts * half :]
    for e in range(experts):
        for j in range(chips):
            at = e * half + j * rows
            out_ref[j, e * rows : (e + 1) * rows, :] = out[at : at + rows].astype(out_ref.dtype)


def sharded_basis_shards(
    tokens, expert_ids, gate_codes, gate_weight, up_weight, down_weight, target_basis
):
    rows, width = tokens.shape
    devices = lax.axis_size("expert")
    chips = devices // CORES
    experts = devices // SLICES
    half = chips * rows
    span = width // chips
    hidden_units = gate_weight.shape[2]
    shard, rank = target_basis.shape
    index = lax.axis_index("expert").astype(jnp.int32)
    chip = (index // CORES).reshape(1)
    core = (index % CORES).reshape(1)
    groups = [list(range(c, devices, CORES)) for c in range(CORES)]

    def swap(x, step):
        return lax.ppermute(x, "expert", [(i, i ^ step) for i in range(devices)])

    order = sorted(range(chips), key=lambda d: (-(d // (2 * CORES)), d % CORES, -d))
    mine = [swap(tokens, CORES * d) if d else tokens for d in order]
    other = [swap(block, 1) for block in mine]
    other_basis = swap(target_basis, 1)

    vmem = pl.BlockSpec(memory_space=pltpu.VMEM)
    smem = pl.BlockSpec(memory_space=pltpu.SMEM)
    weights = [
        pltpu.with_memory_space_constraint(w, pltpu.HBM)
        for w in (gate_weight, up_weight, down_weight)
    ]
    fetched = pl.pallas_call(
        functools.partial(fetch_kernel, chips),
        out_shape=tuple(pltpu.VMEM(w.shape[1:], w.dtype) for w in weights),
        in_specs=[pl.BlockSpec(memory_space=pltpu.HBM)] * 3,
        out_specs=(vmem,) * 3,
        scratch_shapes=[pltpu.SemaphoreType.DMA((3, chips))],
        compiler_params=pltpu.CompilerParams(vmem_limit_bytes=MIB),
        name="fetch_weights",
    )(*weights)
    part_shape = jax.ShapeDtypeStruct((chips, half, span), jnp.bfloat16)
    mine_part, other_part = pl.pallas_call(
        functools.partial(expert_kernel, order),
        out_shape=(part_shape, part_shape),
        in_specs=[smem] + [vmem] * (2 * chips + 3),
        out_specs=(vmem, vmem),
        scratch_shapes=[pltpu.VMEM((2 * half, width), jnp.bfloat16)],
        compiler_params=pltpu.CompilerParams(vmem_limit_bytes=16 * MIB),
        name="expert_work",
    )(chip, *mine, *other, *fetched)
    from_core = swap(other_part, 1)
    pair_part = (mine_part.astype(jnp.float32) + from_core.astype(jnp.float32)).astype(jnp.bfloat16)
    parts = lax.all_to_all(
        pair_part, "expert", split_axis=0, concat_axis=0, axis_index_groups=groups
    )
    partial = pl.pallas_call(
        functools.partial(basis_kernel, experts),
        out_shape=jax.ShapeDtypeStruct((chips, experts * rows, rank), jnp.float32),
        in_specs=[smem, vmem, vmem, vmem],
        out_specs=vmem,
        scratch_shapes=[pltpu.VMEM((CORES * shard, rank), jnp.bfloat16)],
        compiler_params=pltpu.CompilerParams(vmem_limit_bytes=16 * MIB),
        name="basis_product",
    )(core, parts, target_basis, other_basis)
    returned = lax.all_to_all(
        partial, "expert", split_axis=0, concat_axis=0, axis_index_groups=groups
    )
    projected = jnp.sum(returned, axis=0).reshape(experts, rows, rank)
    codes_float = gate_codes.astype(jnp.float32)
    weights = 2.5 * codes_float / jnp.sum(codes_float, axis=1, keepdims=True)
    chosen = expert_ids[None, :, :] == jnp.arange(experts, dtype=jnp.int32)[:, None, None]
    per_expert = jnp.sum(jnp.where(chosen, weights[None, :, :], 0.0), axis=2)
    return jnp.sum(per_expert[:, :, None] * projected, axis=0).astype(jnp.bfloat16)


def fits(tokens, target_basis):
    rows, width = tokens.shape
    devices = lax.axis_size("expert")
    chips = devices // CORES
    return (
        devices % (CORES * SLICES) == 0
        and chips & (chips - 1) == 0
        and chips <= SLICES
        and rows & (rows - 1) == 0
        and width % (chips * LANES) == 0
        and target_basis.shape[0] * CORES * chips == width
        and target_basis.shape[0] % 16 == 0
    )


def shards(tokens, expert_ids, gate_codes, gate_weight, up_weight, down_weight, target_basis):
    plan = sharded_basis_shards if fits(tokens, target_basis) else general_shards
    return plan(
        tokens, expert_ids, gate_codes, gate_weight, up_weight, down_weight, target_basis
    )


def solution(mesh):
    in_specs = (
        P(("group", "expert"), None),
        P(("group", "expert"), None),
        P(("group", "expert"), None),
        P("expert", None, None),
        P("expert", None, None),
        P("expert", None, None),
        P("expert", None),
    )
    out_specs = P(("group", "expert"), None)
    return jax.shard_map(shards, mesh=mesh, in_specs=in_specs, out_specs=out_specs, check_vma=False)
```

```python
import functools

import jax
import jax.numpy as jnp
from jax import lax
from jax.experimental import pallas as pl
from jax.experimental.pallas import tpu as pltpu
from jax.sharding import PartitionSpec as P

SLICES = 8
CORES = 2
COLUMNS = 2
MAX_PLANES = 4
FETCH_PARTS = 8
LANES = 128
MIB = 1 << 20


def run_expert(received, gate_weight, up_weight, down_weight):
    sources, slots, feature_width = received.shape
    row_block = received.reshape(sources * slots, feature_width)
    gate_act = jnp.dot(row_block, gate_weight[0], preferred_element_type=jnp.float32)
    up_act = jnp.dot(row_block, up_weight[0], preferred_element_type=jnp.float32)
    hidden = (jax.nn.silu(gate_act) * up_act).astype(jnp.bfloat16)
    expert_part = jnp.dot(hidden, down_weight[0], preferred_element_type=jnp.float32).astype(
        jnp.bfloat16
    )
    return expert_part.reshape(sources, slots, feature_width)


def general_shards(
    tokens, expert_ids, gate_codes, gate_weight, up_weight, down_weight, target_basis
):
    token_count, feature_width = tokens.shape
    pick_count = expert_ids.shape[1]
    owner_count = lax.axis_size("expert")
    expert_count = owner_count // SLICES
    capacity = min(token_count, max(2, 5 * token_count * pick_count // (4 * expert_count)))
    rank_width = target_basis.shape[1]
    flat_ids = expert_ids.reshape(-1)
    onehot = (flat_ids[:, None] == jnp.arange(expert_count, dtype=jnp.int32)[None, :]).astype(
        jnp.int32
    )
    before = jnp.cumsum(onehot, axis=0) - onehot
    slot_rank = jnp.sum(before * onehot, axis=1)
    slot_index = flat_ids * capacity + slot_rank
    row_token = jnp.arange(token_count * pick_count, dtype=jnp.int32) // pick_count
    slot_table = (
        jnp.full((expert_count * capacity,), token_count, jnp.int32).at[slot_index].set(row_token)
    )
    padded = jnp.concatenate([tokens, jnp.zeros((1, feature_width), tokens.dtype)], axis=0)
    per_expert_rows = padded[slot_table].reshape(expert_count, 1, capacity, feature_width)
    outgoing = jnp.broadcast_to(per_expert_rows, (expert_count, SLICES, capacity, feature_width))
    outgoing = outgoing.reshape(owner_count, capacity, feature_width)
    full_basis = lax.all_gather(target_basis, "expert", axis=0, tiled=True)
    expert_part = run_expert(
        lax.all_to_all(outgoing, "expert", split_axis=0, concat_axis=0, tiled=True),
        gate_weight,
        up_weight,
        down_weight,
    )
    result = jnp.einsum("skd,dr->skr", expert_part, full_basis, preferred_element_type=jnp.float32)
    returned = lax.all_to_all(result, "expert", split_axis=0, concat_axis=0, tiled=True)
    summed = jnp.sum(returned.reshape(expert_count, SLICES, capacity, rank_width), axis=1)
    projected = summed.reshape(expert_count * capacity, rank_width)[slot_index]
    codes_float = gate_codes.astype(jnp.float32)
    weights = 2.5 * codes_float / jnp.sum(codes_float, axis=1, keepdims=True)
    projected = projected.reshape(token_count, pick_count, rank_width)
    return jnp.sum(weights[:, :, None] * projected, axis=1).astype(jnp.bfloat16)


def fetch_kernel(parts, *refs):
    sources, targets, sems = refs[:3], refs[3:6], refs[6]
    copies = []
    for w in range(3):
        rows = sources[w].shape[1] // parts
        for k in range(parts):
            part = pl.ds(k * rows, rows)
            copy = pltpu.make_async_copy(
                sources[w].at[0, part, :], targets[w].at[part, :], sems.at[w, k]
            )
            copy.start()
            copies.append(copy)
    for copy in copies:
        copy.wait()


def expert_kernel(order, me_ref, *refs):
    planes = len(order)
    count = CORES * COLUMNS * planes
    blocks = refs[:count]
    gate_ref, up_ref, down_ref = refs[count : count + 3]
    pieces = refs[count + 3 : -1]
    x_ref = refs[-1]
    rows, width = blocks[0].shape
    quarter = planes * rows
    total = CORES * COLUMNS * quarter
    span = width // planes
    me = me_ref[0]
    for b, block in enumerate(blocks):
        at = b // planes * quarter + order[b % planes] * rows
        x_ref[at : at + rows, :] = block[...]
    x = x_ref[...]
    gate_act = jnp.dot(x, gate_ref[...], preferred_element_type=jnp.float32)
    up_act = jnp.dot(x, up_ref[...], preferred_element_type=jnp.float32)
    hidden = (gate_act / (1.0 + jnp.exp(-gate_act)) * up_act).astype(jnp.bfloat16)
    to_row = lax.broadcasted_iota(jnp.int32, (total, total), 0)
    from_row = lax.broadcasted_iota(jnp.int32, (total, total), 1)
    wanted = jnp.bitwise_xor(from_row, me * rows)
    plane_order = jnp.where(to_row == wanted, 1.0, 0.0).astype(jnp.bfloat16)
    hidden = jnp.dot(plane_order, hidden, preferred_element_type=jnp.float32).astype(jnp.bfloat16)
    for n, step in enumerate(order):
        at = pl.multiple_of(jnp.bitwise_xor(me, step) * span, LANES)
        out = jnp.dot(hidden, down_ref[:, pl.ds(at, span)], preferred_element_type=jnp.float32)
        out = out.astype(jnp.bfloat16)
        for p, piece in enumerate(pieces):
            piece[n] = out[p * quarter : (p + 1) * quarter]


def stack_kernel(place_ref, *refs):
    shards_in, out_ref = refs[:-1], refs[-1]
    rows = shards_in[0].shape[0]
    for b, shard in enumerate(shards_in):
        at = pl.multiple_of(jnp.bitwise_xor(place_ref[0], b) * rows, rows)
        out_ref[pl.ds(at, rows), :] = shard[...]


def basis_kernel(per, me_ref, *refs):
    planes = (len(refs) - 3) // 2
    parts, basis_ref = refs[:planes], refs[planes]
    outs, s_ref, o_ref = refs[planes + 1 : -2], refs[-2], refs[-1]
    quarter = parts[0].shape[0]
    experts = planes // per
    rows = quarter // planes
    me = me_ref[0]
    for e in range(experts):
        total = parts[e * per][...].astype(jnp.float32)
        for d in range(e * per + 1, (e + 1) * per):
            total += parts[d][...].astype(jnp.float32)
        high = total.astype(jnp.bfloat16)
        low = (total - high.astype(jnp.float32)).astype(jnp.bfloat16)
        at = pl.multiple_of(jnp.bitwise_xor(me // per, e) * quarter, quarter)
        s_ref[pl.ds(at, quarter), :] = high
        s_ref[pl.ds(experts * quarter + at, quarter), :] = low
    out = jnp.dot(s_ref[...], basis_ref[...], preferred_element_type=jnp.float32)
    out = out[: experts * quarter] + out[experts * quarter :]
    for e in range(experts):
        for p in range(planes):
            at = e * quarter + p * rows
            o_ref[p, e * rows : (e + 1) * rows, :] = out[at : at + rows]
    for d in range(planes):
        outs[d][...] = o_ref[jnp.bitwise_xor(me, d)]


def sharded_basis_shards(
    tokens, expert_ids, gate_codes, gate_weight, up_weight, down_weight, target_basis
):
    rows, width = tokens.shape
    devices = lax.axis_size("expert")
    place_count = CORES * COLUMNS
    planes = devices // place_count
    experts = devices // SLICES
    quarter = planes * rows
    span = width // planes
    rank = target_basis.shape[1]
    index = lax.axis_index("expert").astype(jnp.int32)
    plane = jnp.right_shift(index, place_count.bit_length() - 1).reshape(1)
    place = jnp.bitwise_and(index, place_count - 1).reshape(1)
    bf16 = jnp.bfloat16

    def swap(x, step):
        return lax.ppermute(x, "expert", [(i, i ^ step) for i in range(devices)])

    def core_swap(x):
        return swap(x, 1)

    def column_swap(x):
        return swap(x, CORES)

    def plane_swap(x, step):
        return swap(x, place_count * step) if step else x

    vmem = pl.BlockSpec(memory_space=pltpu.VMEM)
    smem = pl.BlockSpec(memory_space=pltpu.SMEM)

    order = list(range(planes))[::-1]
    near = [plane_swap(tokens, d) for d in order]
    blocks = near + [column_swap(block) for block in near]
    blocks = blocks + [core_swap(block) for block in blocks]

    weights = [
        pltpu.with_memory_space_constraint(w, pltpu.HBM)
        for w in (gate_weight, up_weight, down_weight)
    ]
    fetched = pl.pallas_call(
        functools.partial(fetch_kernel, FETCH_PARTS),
        out_shape=tuple(pltpu.VMEM(w.shape[1:], w.dtype) for w in weights),
        in_specs=[pl.BlockSpec(memory_space=pltpu.HBM)] * 3,
        out_specs=(vmem,) * 3,
        scratch_shapes=[pltpu.SemaphoreType.DMA((3, FETCH_PARTS))],
        compiler_params=pltpu.CompilerParams(vmem_limit_bytes=MIB),
        name="fetch_weights",
    )(*weights)
    piece = jax.ShapeDtypeStruct((planes, quarter, span), bf16)
    pieces = pl.pallas_call(
        functools.partial(expert_kernel, order),
        out_shape=(piece,) * place_count,
        in_specs=[smem] + [vmem] * (len(blocks) + 3),
        out_specs=(vmem,) * place_count,
        scratch_shapes=[pltpu.VMEM((place_count * quarter, width), bf16)],
        compiler_params=pltpu.CompilerParams(vmem_limit_bytes=16 * MIB),
        name="expert_work",
    )(plane, *blocks, *fetched)

    basis_shards = [target_basis, core_swap(target_basis)]
    column_basis = column_swap(target_basis)
    basis_shards += [column_basis, core_swap(column_basis)]
    basis = pl.pallas_call(
        stack_kernel,
        out_shape=jax.ShapeDtypeStruct((width // planes, rank), bf16),
        in_specs=[smem] + [vmem] * place_count,
        out_specs=vmem,
        compiler_params=pltpu.CompilerParams(vmem_limit_bytes=8 * MIB),
        name="stack_basis",
    )(place, *basis_shards)

    own_own, own_far, other_own, other_far = pieces
    other_far = core_swap(other_far)
    other_own = core_swap(other_own)
    parts = {}
    for n, d in enumerate(order):
        pair = (own_far[n].astype(jnp.float32) + other_far[n].astype(jnp.float32)).astype(bf16)
        crossed = column_swap(pair)
        total = own_own[n].astype(jnp.float32) + other_own[n].astype(jnp.float32)
        total = total + crossed.astype(jnp.float32)
        parts[d] = plane_swap(total.astype(bf16), d) if d else total
    out_piece = jax.ShapeDtypeStruct((experts * rows, rank), jnp.float32)
    partial = pl.pallas_call(
        functools.partial(basis_kernel, SLICES // place_count),
        out_shape=(out_piece,) * planes,
        in_specs=[smem] + [vmem] * (planes + 1),
        out_specs=(vmem,) * planes,
        scratch_shapes=[
            pltpu.VMEM((2 * experts * quarter, span), bf16),
            pltpu.VMEM((planes, experts * rows, rank), jnp.float32),
        ],
        compiler_params=pltpu.CompilerParams(vmem_limit_bytes=16 * MIB),
        name="basis_product",
    )(plane, *[parts[d] for d in range(planes)], basis)
    projected = sum(plane_swap(partial[d], d) for d in order)
    projected = projected.reshape(experts, rows, rank)
    codes_float = gate_codes.astype(jnp.float32)
    gates = 2.5 * codes_float / jnp.sum(codes_float, axis=1, keepdims=True)
    chosen = expert_ids[None, :, :] == jnp.arange(experts, dtype=jnp.int32)[:, None, None]
    per_expert = jnp.sum(jnp.where(chosen, gates[None, :, :], 0.0), axis=2)
    return jnp.sum(per_expert[:, :, None] * projected, axis=0).astype(bf16)


def fits(tokens, target_basis):
    rows, width = tokens.shape
    devices = lax.axis_size("expert")
    planes = devices // (CORES * COLUMNS)
    return (
        devices % SLICES == 0
        and SLICES % (CORES * COLUMNS) == 0
        and planes & (planes - 1) == 0
        and 1 < planes <= MAX_PLANES
        and rows & (rows - 1) == 0
        and planes * rows % 16 == 0
        and width % (planes * LANES) == 0
        and target_basis.shape[0] * devices == width
        and target_basis.shape[0] % 16 == 0
    )


def shards(tokens, expert_ids, gate_codes, gate_weight, up_weight, down_weight, target_basis):
    plan = sharded_basis_shards if fits(tokens, target_basis) else general_shards
    return plan(
        tokens, expert_ids, gate_codes, gate_weight, up_weight, down_weight, target_basis
    )


def solution(mesh):
    in_specs = (
        P(("group", "expert"), None),
        P(("group", "expert"), None),
        P(("group", "expert"), None),
        P("expert", None, None),
        P("expert", None, None),
        P("expert", None, None),
        P("expert", None),
    )
    out_specs = P(("group", "expert"), None)
    return jax.shard_map(shards, mesh=mesh, in_specs=in_specs, out_specs=out_specs, check_vma=False)
```

```python
import functools

import jax
import jax.numpy as jnp
from jax import lax
from jax.experimental import pallas as pl
from jax.experimental.pallas import tpu as pltpu
from jax.sharding import PartitionSpec as P


SLICES = 8
CORES = 2
COLUMNS = 2
MAX_PLANES = 4
FETCH_PARTS = 8
LANES = 128
MIB = 1 << 20


def run_expert(received, gate_weight, up_weight, down_weight):
    sources, slots, feature_width = received.shape
    row_block = received.reshape(sources * slots, feature_width)
    gate_act = jnp.dot(row_block, gate_weight[0], preferred_element_type=jnp.float32)
    up_act = jnp.dot(row_block, up_weight[0], preferred_element_type=jnp.float32)
    hidden = (jax.nn.silu(gate_act) * up_act).astype(jnp.bfloat16)
    expert_part = jnp.dot(hidden, down_weight[0], preferred_element_type=jnp.float32).astype(
        jnp.bfloat16
    )
    return expert_part.reshape(sources, slots, feature_width)


def general_shards(
    tokens, expert_ids, gate_codes, gate_weight, up_weight, down_weight, target_basis
):
    token_count, feature_width = tokens.shape
    pick_count = expert_ids.shape[1]
    owner_count = lax.axis_size("expert")
    expert_count = owner_count // SLICES
    capacity = min(token_count, max(2, 5 * token_count * pick_count // (4 * expert_count)))
    rank_width = target_basis.shape[1]
    flat_ids = expert_ids.reshape(-1)
    onehot = (flat_ids[:, None] == jnp.arange(expert_count, dtype=jnp.int32)[None, :]).astype(
        jnp.int32
    )
    before = jnp.cumsum(onehot, axis=0) - onehot
    slot_rank = jnp.sum(before * onehot, axis=1)
    slot_index = flat_ids * capacity + slot_rank
    row_token = jnp.arange(token_count * pick_count, dtype=jnp.int32) // pick_count
    slot_table = (
        jnp.full((expert_count * capacity,), token_count, jnp.int32).at[slot_index].set(row_token)
    )
    padded = jnp.concatenate([tokens, jnp.zeros((1, feature_width), tokens.dtype)], axis=0)
    per_expert_rows = padded[slot_table].reshape(expert_count, 1, capacity, feature_width)
    outgoing = jnp.broadcast_to(per_expert_rows, (expert_count, SLICES, capacity, feature_width))
    outgoing = outgoing.reshape(owner_count, capacity, feature_width)
    full_basis = lax.all_gather(target_basis, "expert", axis=0, tiled=True)
    expert_part = run_expert(
        lax.all_to_all(outgoing, "expert", split_axis=0, concat_axis=0, tiled=True),
        gate_weight,
        up_weight,
        down_weight,
    )
    result = jnp.einsum("skd,dr->skr", expert_part, full_basis, preferred_element_type=jnp.float32)
    returned = lax.all_to_all(result, "expert", split_axis=0, concat_axis=0, tiled=True)
    summed = jnp.sum(returned.reshape(expert_count, SLICES, capacity, rank_width), axis=1)
    projected = summed.reshape(expert_count * capacity, rank_width)[slot_index]
    codes_float = gate_codes.astype(jnp.float32)
    weights = 2.5 * codes_float / jnp.sum(codes_float, axis=1, keepdims=True)
    projected = projected.reshape(token_count, pick_count, rank_width)
    return jnp.sum(weights[:, :, None] * projected, axis=1).astype(jnp.bfloat16)


def fetch_kernel(index_ref, *refs):
    del index_ref
    sems = refs[-1]
    count, parts = sems.shape
    copies = []
    for k in range(parts):
        for w in range(count):
            source, target = refs[w], refs[count + w]
            rows = target.shape[0] // parts
            part = pl.ds(k * rows, rows)
            copies.append(
                pltpu.make_async_copy(source.at[0, part, :], target.at[part, :], sems.at[w, k])
            )
            copies[-1].start()
    for copy in copies:
        copy.wait()


def stack_tokens_kernel(rows_at, *refs):
    for at, block in zip(rows_at, refs[:-1]):
        rows = block.shape[0]
        refs[-1][at : at + rows, :] = block[...]


def plane_of(index):
    return jnp.right_shift(index, (CORES * COLUMNS).bit_length() - 1)


def place_of(index):
    return jnp.bitwise_and(index, CORES * COLUMNS - 1)


def expert_kernel(order, index_ref, *refs):
    places = CORES * COLUMNS
    stacks = refs[:places]
    gate_ref, up_ref, down_ref = refs[places : places + 3]
    pieces = refs[places + 3 : -1]
    x_ref = refs[-1]
    planes = len(order)
    quarter, width = stacks[0].shape
    rows = quarter // planes
    total = places * quarter
    span = width // planes
    me = plane_of(index_ref[0])
    for b, stack in enumerate(stacks):
        x_ref[b * quarter : (b + 1) * quarter, :] = stack[...]
    x = x_ref[...]
    gate_act = jnp.dot(x, gate_ref[...], preferred_element_type=jnp.float32)
    up_act = jnp.dot(x, up_ref[...], preferred_element_type=jnp.float32)
    hidden = (gate_act / (1.0 + jnp.exp(-gate_act)) * up_act).astype(jnp.bfloat16)
    to_row = lax.broadcasted_iota(jnp.int32, (total, total), 0)
    from_row = lax.broadcasted_iota(jnp.int32, (total, total), 1)
    wanted = jnp.bitwise_xor(from_row, me * rows)
    plane_order = jnp.where(to_row == wanted, 1.0, 0.0).astype(jnp.bfloat16)
    hidden = jnp.dot(plane_order, hidden, preferred_element_type=jnp.float32).astype(jnp.bfloat16)
    for n, step in enumerate(order):
        at = pl.multiple_of(jnp.bitwise_xor(me, step) * span, LANES)
        out = jnp.dot(hidden, down_ref[:, pl.ds(at, span)], preferred_element_type=jnp.float32)
        out = out.astype(jnp.bfloat16)
        for p, piece in enumerate(pieces):
            piece[n] = out[p * quarter : (p + 1) * quarter]


def stack_kernel(index_ref, *refs):
    shards_in, out_ref = refs[:-1], refs[-1]
    rows = shards_in[0].shape[0]
    for b, shard in enumerate(shards_in):
        at = pl.multiple_of(jnp.bitwise_xor(place_of(index_ref[0]), b) * rows, rows)
        out_ref[pl.ds(at, rows), :] = shard[...]


def part_total(at, own_ref, other_ref, crossed_ref):
    total = own_ref[at].astype(jnp.float32) + other_ref[at].astype(jnp.float32)
    first = own_ref.shape[0] - crossed_ref.shape[0]
    return total + crossed_ref[max(at - first, 0)].astype(jnp.float32)


def total_kernel(at, own_ref, other_ref, crossed_ref, out_ref):
    out_ref[...] = part_total(at, own_ref, other_ref, crossed_ref).astype(out_ref.dtype)


def basis_kernel(per, index_ref, own_ref, other_ref, crossed_ref, *refs):
    planes = (len(refs) - 2) // 2
    parts, basis_ref = refs[: planes - 1], refs[planes - 1]
    outs, s_ref, o_ref = refs[planes:-2], refs[-2], refs[-1]
    quarter = crossed_ref.shape[1]
    experts = planes // per
    rows = quarter // planes
    me = plane_of(index_ref[0])
    for e in range(experts):
        total = part_total(planes - 1, own_ref, other_ref, crossed_ref) if e == 0 else 0.0
        for d in range(max(1, e * per), (e + 1) * per):
            total += parts[d - 1][...].astype(jnp.float32)
        high = total.astype(jnp.bfloat16)
        low = (total - high.astype(jnp.float32)).astype(jnp.bfloat16)
        at = pl.multiple_of(jnp.bitwise_xor(me // per, e) * quarter, quarter)
        s_ref[pl.ds(at, quarter), :] = high
        s_ref[pl.ds(experts * quarter + at, quarter), :] = low
    out = jnp.dot(s_ref[...], basis_ref[...], preferred_element_type=jnp.float32)
    out = out[: experts * quarter] + out[experts * quarter :]
    for e in range(experts):
        for p in range(planes):
            at = e * quarter + p * rows
            o_ref[p, e * rows : (e + 1) * rows, :] = out[at : at + rows]
    for d in range(planes):
        outs[d][...] = o_ref[jnp.bitwise_xor(me, d)]


def sharded_basis_shards(
    tokens, expert_ids, gate_codes, gate_weight, up_weight, down_weight, target_basis
):
    rows, width = tokens.shape
    devices = lax.axis_size("expert")
    place_count = CORES * COLUMNS
    planes = devices // place_count
    experts = devices // SLICES
    quarter = planes * rows
    span = width // planes
    rank = target_basis.shape[1]
    index = lax.axis_index("expert").astype(jnp.int32).reshape(1)
    bf16 = jnp.bfloat16

    def swap(x, step):
        return lax.ppermute(x, "expert", [(i, i ^ step) for i in range(devices)])

    def core_swap(x):
        return swap(x, 1)

    def column_swap(x):
        return swap(x, CORES)

    def plane_swap(x, step):
        return swap(x, place_count * step) if step else x

    vmem = pl.BlockSpec(memory_space=pltpu.VMEM)
    smem = pl.BlockSpec(memory_space=pltpu.SMEM)

    order = sorted(range(planes), key=lambda d: (d < planes // 2, d))
    order = order[: planes // 2] + order[: planes // 2 - 1 : -1]
    near = {d: plane_swap(tokens, d) for d in order}
    far = {d: column_swap(near[d]) for d in order}
    stacks = []
    for blocks in (near, far):
        stacks.append(
            pl.pallas_call(
                functools.partial(stack_tokens_kernel, [d * rows for d in order]),
                out_shape=jax.ShapeDtypeStruct((quarter, width), bf16),
                in_specs=[vmem] * planes,
                out_specs=vmem,
                compiler_params=pltpu.CompilerParams(vmem_limit_bytes=4 * MIB),
                name="stack_tokens",
            )(*[blocks[d] for d in order])
        )
    stacks += [core_swap(stack) for stack in stacks]

    basis_shards = [target_basis, core_swap(target_basis)]
    column_basis = column_swap(target_basis)
    basis_shards += [column_basis, core_swap(column_basis)]

    fetched = []
    for group in ((gate_weight, up_weight), (down_weight,)):
        group = [pltpu.with_memory_space_constraint(w, pltpu.HBM) for w in group]
        fetched += pl.pallas_call(
            fetch_kernel,
            out_shape=tuple(pltpu.VMEM(w.shape[1:], w.dtype) for w in group),
            in_specs=[smem] + [pl.BlockSpec(memory_space=pltpu.HBM)] * len(group),
            out_specs=(vmem,) * len(group),
            scratch_shapes=[pltpu.SemaphoreType.DMA((len(group), FETCH_PARTS))],
            compiler_params=pltpu.CompilerParams(vmem_limit_bytes=MIB),
        )(index, *group)
    fetched = [pltpu.with_memory_space_constraint(w, pltpu.VMEM) for w in fetched]
    piece = jax.ShapeDtypeStruct((planes, quarter, span), bf16)
    pieces = pl.pallas_call(
        functools.partial(expert_kernel, order),
        out_shape=(piece,) * place_count,
        in_specs=[smem] + [vmem] * (place_count + 3),
        out_specs=(vmem,) * place_count,
        scratch_shapes=[pltpu.VMEM((place_count * quarter, width), bf16)],
        compiler_params=pltpu.CompilerParams(vmem_limit_bytes=16 * MIB),
        name="expert_work",
    )(index, *stacks, *fetched)

    basis = pl.pallas_call(
        stack_kernel,
        out_shape=jax.ShapeDtypeStruct((width // planes, rank), bf16),
        in_specs=[smem] + [vmem] * place_count,
        out_specs=vmem,
        compiler_params=pltpu.CompilerParams(vmem_limit_bytes=8 * MIB),
        name="stack_basis",
    )(index, *basis_shards)

    own_own, own_far, other_own, other_far = pieces
    other_far = core_swap(other_far)
    other_own = core_swap(other_own)
    pairs = (own_far.astype(jnp.float32) + other_far.astype(jnp.float32)).astype(bf16)
    crossed = {}
    for n, d in enumerate(order):
        if d >= planes // 2:
            crossed[d] = column_swap(pairs[n : n + 1])
    rest = column_swap(pairs[len(crossed) :])
    crossed.update({d: rest for d in range(planes // 2)})
    parts = []
    for d in range(1, planes):
        total = pl.pallas_call(
            functools.partial(total_kernel, order.index(d)),
            out_shape=jax.ShapeDtypeStruct((quarter, span), bf16),
            in_specs=[vmem] * 3,
            out_specs=vmem,
            compiler_params=pltpu.CompilerParams(vmem_limit_bytes=4 * MIB),
        )(own_own, other_own, crossed[d])
        parts.append(plane_swap(total, d))
    out_piece = jax.ShapeDtypeStruct((experts * rows, rank), jnp.float32)
    partial = pl.pallas_call(
        functools.partial(basis_kernel, SLICES // place_count),
        out_shape=(out_piece,) * planes,
        in_specs=[smem] + [vmem] * (planes + 3),
        out_specs=(vmem,) * planes,
        scratch_shapes=[
            pltpu.VMEM((2 * experts * quarter, span), bf16),
            pltpu.VMEM((planes, experts * rows, rank), jnp.float32),
        ],
        compiler_params=pltpu.CompilerParams(vmem_limit_bytes=16 * MIB),
        name="basis_product",
    )(index, own_own, other_own, crossed[0], *parts, basis)
    projected = sum(plane_swap(partial[d], d) for d in order)
    projected = projected.reshape(experts, rows, rank)
    codes_float = gate_codes.astype(jnp.float32)
    gates = 2.5 * codes_float / jnp.sum(codes_float, axis=1, keepdims=True)
    chosen = expert_ids[None, :, :] == jnp.arange(experts, dtype=jnp.int32)[:, None, None]
    per_expert = jnp.sum(jnp.where(chosen, gates[None, :, :], 0.0), axis=2)
    return jnp.sum(per_expert[:, :, None] * projected, axis=0).astype(bf16)


def fits(tokens, target_basis):
    rows, width = tokens.shape
    devices = lax.axis_size("expert")
    planes = devices // (CORES * COLUMNS)
    return (
        devices % SLICES == 0
        and SLICES % (CORES * COLUMNS) == 0
        and planes & (planes - 1) == 0
        and 1 < planes <= MAX_PLANES
        and rows & (rows - 1) == 0
        and planes * rows % 16 == 0
        and width % (planes * LANES) == 0
        and target_basis.shape[0] * devices == width
        and target_basis.shape[0] % 16 == 0
    )


def shards(tokens, expert_ids, gate_codes, gate_weight, up_weight, down_weight, target_basis):
    plan = sharded_basis_shards if fits(tokens, target_basis) else general_shards
    return plan(tokens, expert_ids, gate_codes, gate_weight, up_weight, down_weight, target_basis)


def solution(mesh):
    in_specs = (
        P(("group", "expert"), None),
        P(("group", "expert"), None),
        P(("group", "expert"), None),
        P("expert", None, None),
        P("expert", None, None),
        P("expert", None, None),
        P("expert", None),
    )
    out_specs = P(("group", "expert"), None)
    return jax.shard_map(shards, mesh=mesh, in_specs=in_specs, out_specs=out_specs, check_vma=False)
```

```python
import functools

import jax
import jax.numpy as jnp
from jax import lax
from jax.experimental import pallas as pl
from jax.experimental.pallas import tpu as pltpu
from jax.sharding import PartitionSpec as P


SLICES = 8
CORES = 2
COLUMNS = 2
MAX_PLANES = 4
FETCH_PARTS = 8
LANES = 128
MIB = 1 << 20


def run_expert(received, gate_weight, up_weight, down_weight):
    sources, slots, feature_width = received.shape
    row_block = received.reshape(sources * slots, feature_width)
    gate_act = jnp.dot(row_block, gate_weight[0], preferred_element_type=jnp.float32)
    up_act = jnp.dot(row_block, up_weight[0], preferred_element_type=jnp.float32)
    hidden = (jax.nn.silu(gate_act) * up_act).astype(jnp.bfloat16)
    expert_part = jnp.dot(hidden, down_weight[0], preferred_element_type=jnp.float32).astype(
        jnp.bfloat16
    )
    return expert_part.reshape(sources, slots, feature_width)


def general_shards(
    tokens, expert_ids, gate_codes, gate_weight, up_weight, down_weight, target_basis
):
    token_count, feature_width = tokens.shape
    pick_count = expert_ids.shape[1]
    owner_count = lax.axis_size("expert")
    expert_count = owner_count // SLICES
    capacity = min(token_count, max(2, 5 * token_count * pick_count // (4 * expert_count)))
    rank_width = target_basis.shape[1]
    flat_ids = expert_ids.reshape(-1)
    onehot = (flat_ids[:, None] == jnp.arange(expert_count, dtype=jnp.int32)[None, :]).astype(
        jnp.int32
    )
    before = jnp.cumsum(onehot, axis=0) - onehot
    slot_rank = jnp.sum(before * onehot, axis=1)
    slot_index = flat_ids * capacity + slot_rank
    row_token = jnp.arange(token_count * pick_count, dtype=jnp.int32) // pick_count
    slot_table = (
        jnp.full((expert_count * capacity,), token_count, jnp.int32).at[slot_index].set(row_token)
    )
    padded = jnp.concatenate([tokens, jnp.zeros((1, feature_width), tokens.dtype)], axis=0)
    per_expert_rows = padded[slot_table].reshape(expert_count, 1, capacity, feature_width)
    outgoing = jnp.broadcast_to(per_expert_rows, (expert_count, SLICES, capacity, feature_width))
    outgoing = outgoing.reshape(owner_count, capacity, feature_width)
    full_basis = lax.all_gather(target_basis, "expert", axis=0, tiled=True)
    expert_part = run_expert(
        lax.all_to_all(outgoing, "expert", split_axis=0, concat_axis=0, tiled=True),
        gate_weight,
        up_weight,
        down_weight,
    )
    result = jnp.einsum("skd,dr->skr", expert_part, full_basis, preferred_element_type=jnp.float32)
    returned = lax.all_to_all(result, "expert", split_axis=0, concat_axis=0, tiled=True)
    summed = jnp.sum(returned.reshape(expert_count, SLICES, capacity, rank_width), axis=1)
    projected = summed.reshape(expert_count * capacity, rank_width)[slot_index]
    codes_float = gate_codes.astype(jnp.float32)
    weights = 2.5 * codes_float / jnp.sum(codes_float, axis=1, keepdims=True)
    projected = projected.reshape(token_count, pick_count, rank_width)
    return jnp.sum(weights[:, :, None] * projected, axis=1).astype(jnp.bfloat16)


def fetch_kernel(parts, index_ref, *refs):
    del index_ref
    sources, targets, sems = refs[: len(parts)], refs[len(parts) : -1], refs[-1]
    copies = []
    for source, target, count in zip(sources, targets, parts):
        rows = target.shape[0] // count
        for k in range(count):
            block = pl.ds(k * rows, rows)
            sem = sems.at[len(copies)]
            copies.append(pltpu.make_async_copy(source.at[block, :], target.at[block, :], sem))
            copies[-1].start()
    for copy in copies:
        copy.wait()


def split_kernel(source, *refs):
    targets, sems = refs[:-1], refs[-1]
    copies, at = [], 0
    for n, target in enumerate(targets):
        rows = target.shape[0]
        copies.append(pltpu.make_async_copy(source.at[pl.ds(at, rows), :], target, sems.at[n]))
        copies[n].start()
        at += rows
    for copy in copies:
        copy.wait()


def stack_blocks_kernel(*refs):
    for n, block in enumerate(refs[:-1]):
        refs[-1][n] = block[...]


def stack_rows_kernel(sources, *refs):
    out_ref = refs[-1]
    for n, (ref, at) in enumerate(sources):
        block = refs[ref][...] if at is None else refs[ref][at]
        rows = block.shape[0]
        out_ref[n * rows : (n + 1) * rows, :] = block


def plane_of(index):
    return jnp.right_shift(index, (CORES * COLUMNS).bit_length() - 1)


def place_of(index):
    return jnp.bitwise_and(index, CORES * COLUMNS - 1)


def expert_kernel(order, index_ref, *refs):
    places = CORES * COLUMNS
    stacks = refs[:places]
    gate_ref, up_ref, down_ref = refs[places : places + 3]
    pieces = refs[places + 3 : -1]
    x_ref = refs[-1]
    planes = len(order)
    quarter, width = stacks[0].shape
    rows = quarter // planes
    total = places * quarter
    span = width // planes
    me = plane_of(index_ref[0])
    for b, stack in enumerate(stacks):
        x_ref[b * quarter : (b + 1) * quarter, :] = stack[...]
    x = x_ref[...]
    gate_act = jnp.dot(x, gate_ref[...], preferred_element_type=jnp.float32)
    up_act = jnp.dot(x, up_ref[...], preferred_element_type=jnp.float32)
    hidden = (gate_act / (1.0 + jnp.exp(-gate_act)) * up_act).astype(jnp.bfloat16)
    to_row = lax.broadcasted_iota(jnp.int32, (total, total), 0)
    from_row = lax.broadcasted_iota(jnp.int32, (total, total), 1)
    wanted = jnp.bitwise_xor(from_row, me * rows)
    plane_order = jnp.where(to_row == wanted, 1.0, 0.0).astype(jnp.bfloat16)
    hidden = jnp.dot(plane_order, hidden, preferred_element_type=jnp.float32).astype(jnp.bfloat16)
    for n, step in enumerate(order):
        at = pl.multiple_of(jnp.bitwise_xor(me, step) * span, LANES)
        out = jnp.dot(hidden, down_ref[:, pl.ds(at, span)], preferred_element_type=jnp.float32)
        out = out.astype(jnp.bfloat16)
        for p, piece in enumerate(pieces):
            piece[n] = out[p * quarter : (p + 1) * quarter]


def stack_kernel(shard, index_ref, *refs):
    out_ref = refs[-1]
    place = place_of(index_ref[0])
    taken = 0
    for part in refs[:-1]:
        rows = part.shape[0]
        at = jnp.bitwise_xor(place, taken // shard) * shard + taken % shard
        out_ref[pl.ds(pl.multiple_of(at, 16), rows), :] = part[...]
        taken += rows


def part_total(at, own_ref, other_ref, crossed_ref):
    total = own_ref[at].astype(jnp.float32) + other_ref[at].astype(jnp.float32)
    return total + crossed_ref[at % crossed_ref.shape[0]].astype(jnp.float32)


def total_kernel(at, own_ref, other_ref, crossed_ref, out_ref):
    out_ref[...] = part_total(at, own_ref, other_ref, crossed_ref).astype(out_ref.dtype)


def basis_kernel(per, index_ref, own_ref, other_ref, crossed_ref, *refs):
    planes = (len(refs) - 2) // 2
    parts, basis_ref = refs[: planes - 1], refs[planes - 1]
    outs, s_ref, o_ref = refs[planes:-2], refs[-2], refs[-1]
    quarter = crossed_ref.shape[1]
    experts = planes // per
    rows = quarter // planes
    me = plane_of(index_ref[0])
    for e in range(experts):
        total = part_total(planes - 1, own_ref, other_ref, crossed_ref) if e == 0 else 0.0
        for d in range(max(1, e * per), (e + 1) * per):
            total += parts[d - 1][...].astype(jnp.float32)
        high = total.astype(jnp.bfloat16)
        low = (total - high.astype(jnp.float32)).astype(jnp.bfloat16)
        at = pl.multiple_of(jnp.bitwise_xor(me // per, e) * quarter, quarter)
        s_ref[pl.ds(at, quarter), :] = high
        s_ref[pl.ds(experts * quarter + at, quarter), :] = low
    out = jnp.dot(s_ref[...], basis_ref[...], preferred_element_type=jnp.float32)
    out = out[: experts * quarter] + out[experts * quarter :]
    for e in range(experts):
        for p in range(planes):
            at = e * quarter + p * rows
            o_ref[p, e * rows : (e + 1) * rows, :] = out[at : at + rows]
    for d in range(planes):
        outs[d][...] = o_ref[jnp.bitwise_xor(me, d)]


def sharded_basis_shards(
    tokens, expert_ids, gate_codes, gate_weight, up_weight, down_weight, target_basis
):
    rows, width = tokens.shape
    devices = lax.axis_size("expert")
    place_count = CORES * COLUMNS
    planes = devices // place_count
    experts = devices // SLICES
    quarter = planes * rows
    span = width // planes
    rank = target_basis.shape[1]
    index = lax.axis_index("expert").astype(jnp.int32).reshape(1)
    bf16 = jnp.bfloat16

    def swap(x, step):
        return lax.ppermute(x, "expert", [(i, i ^ step) for i in range(devices)])

    def core_swap(x):
        return swap(x, 1)

    def column_swap(x):
        return swap(x, CORES)

    def plane_swap(x, step):
        return swap(x, place_count * step) if step else x

    vmem = pl.BlockSpec(memory_space=pltpu.VMEM)
    smem = pl.BlockSpec(memory_space=pltpu.SMEM)

    order = sorted(range(planes), key=lambda d: (d < planes // 2, d))
    order = order[: planes // 2] + order[: planes // 2 - 1 : -1]
    near = {d: plane_swap(tokens, d) for d in order}
    own_far = column_swap(tokens)

    hbm = pl.BlockSpec(memory_space=pltpu.HBM)

    def fetch(parts, *operands):
        operands = [pltpu.with_memory_space_constraint(x, pltpu.HBM) for x in operands]
        out = pl.pallas_call(
            functools.partial(fetch_kernel, parts),
            out_shape=tuple(pltpu.VMEM(x.shape, x.dtype) for x in operands),
            in_specs=[smem] + [hbm] * len(operands),
            out_specs=(vmem,) * len(operands),
            scratch_shapes=[pltpu.SemaphoreType.DMA((sum(parts),))],
            compiler_params=pltpu.CompilerParams(vmem_limit_bytes=MIB),
        )(index, *operands)
        return [pltpu.with_memory_space_constraint(x, pltpu.VMEM) for x in out]

    gate, up, own = fetch((FETCH_PARTS, FETCH_PARTS, 1), gate_weight[0], up_weight[0], tokens)
    (down,) = fetch((FETCH_PARTS,), down_weight[0])

    def stack(kernel, shape, blocks):
        return pl.pallas_call(
            kernel,
            out_shape=jax.ShapeDtypeStruct(shape, bf16),
            in_specs=[vmem] * len(blocks),
            out_specs=vmem,
            compiler_params=pltpu.CompilerParams(vmem_limit_bytes=4 * MIB),
            name="stack_tokens",
        )(*blocks)

    relayed = stack(
        stack_blocks_kernel, (planes - 1, rows, width), [near[d] for d in range(1, planes)]
    )
    relayed = column_swap(relayed)
    stacks = [
        stack(
            functools.partial(stack_rows_kernel, [(d, None) for d in range(planes)]),
            (quarter, width),
            [own] + [near[d] for d in range(1, planes)],
        ),
        stack(
            functools.partial(
                stack_rows_kernel, [(0, None)] + [(1, d) for d in range(planes - 1)]
            ),
            (quarter, width),
            [own_far, relayed],
        ),
    ]
    stacks += [core_swap(tokens_stack) for tokens_stack in stacks]

    shard = target_basis.shape[0]
    late = shard // 64 * 16
    basis_parts = pl.pallas_call(
        split_kernel,
        out_shape=tuple(pltpu.VMEM((n, rank), bf16) for n in (shard - late, late)),
        in_specs=[hbm],
        out_specs=(vmem,) * 2,
        scratch_shapes=[pltpu.SemaphoreType.DMA((2,))],
        compiler_params=pltpu.CompilerParams(vmem_limit_bytes=MIB),
        name="split_basis",
    )(pltpu.with_memory_space_constraint(target_basis, pltpu.HBM))
    column_parts = [column_swap(x) for x in basis_parts]
    basis_shards = [
        *basis_parts, core_swap(target_basis), *column_parts, *[core_swap(x) for x in column_parts]
    ]

    piece = jax.ShapeDtypeStruct((planes, quarter, span), bf16)
    pieces = pl.pallas_call(
        functools.partial(expert_kernel, order),
        out_shape=(piece,) * place_count,
        in_specs=[smem] + [vmem] * (place_count + 3),
        out_specs=(vmem,) * place_count,
        scratch_shapes=[pltpu.VMEM((place_count * quarter, width), bf16)],
        compiler_params=pltpu.CompilerParams(vmem_limit_bytes=16 * MIB),
        name="expert_work",
    )(index, *stacks, gate, up, down)

    basis = pl.pallas_call(
        functools.partial(stack_kernel, shard),
        out_shape=jax.ShapeDtypeStruct((width // planes, rank), bf16),
        in_specs=[smem] + [vmem] * len(basis_shards),
        out_specs=vmem,
        compiler_params=pltpu.CompilerParams(vmem_limit_bytes=8 * MIB),
        name="stack_basis",
    )(index, *basis_shards)

    own_own, own_far, other_own, other_far = pieces
    other_far = core_swap(other_far)
    other_own = core_swap(other_own)
    pairs = (own_far.astype(jnp.float32) + other_far.astype(jnp.float32)).astype(bf16)
    far_count = planes // 2
    crossed = [column_swap(pairs[:far_count]), column_swap(pairs[far_count:])]
    parts = []
    for d in range(1, planes):
        total = pl.pallas_call(
            functools.partial(total_kernel, order.index(d)),
            out_shape=jax.ShapeDtypeStruct((quarter, span), bf16),
            in_specs=[vmem] * 3,
            out_specs=vmem,
            compiler_params=pltpu.CompilerParams(vmem_limit_bytes=4 * MIB),
        )(own_own, other_own, crossed[d < far_count])
        parts.append(plane_swap(total, d))
    out_piece = jax.ShapeDtypeStruct((experts * rows, rank), jnp.float32)
    partial = pl.pallas_call(
        functools.partial(basis_kernel, SLICES // place_count),
        out_shape=(out_piece,) * planes,
        in_specs=[smem] + [vmem] * (planes + 3),
        out_specs=(vmem,) * planes,
        scratch_shapes=[
            pltpu.VMEM((2 * experts * quarter, span), bf16),
            pltpu.VMEM((planes, experts * rows, rank), jnp.float32),
        ],
        compiler_params=pltpu.CompilerParams(vmem_limit_bytes=16 * MIB),
        name="basis_product",
    )(index, own_own, other_own, crossed[1], *parts, basis)
    projected = sum(plane_swap(partial[d], d) for d in order)
    projected = projected.reshape(experts, rows, rank)
    codes_float = gate_codes.astype(jnp.float32)
    gates = 2.5 * codes_float / jnp.sum(codes_float, axis=1, keepdims=True)
    chosen = expert_ids[None, :, :] == jnp.arange(experts, dtype=jnp.int32)[:, None, None]
    per_expert = jnp.sum(jnp.where(chosen, gates[None, :, :], 0.0), axis=2)
    return jnp.sum(per_expert[:, :, None] * projected, axis=0).astype(bf16)


def fits(tokens, target_basis):
    rows, width = tokens.shape
    devices = lax.axis_size("expert")
    planes = devices // (CORES * COLUMNS)
    return (
        devices % SLICES == 0
        and SLICES % (CORES * COLUMNS) == 0
        and planes & (planes - 1) == 0
        and 1 < planes <= MAX_PLANES
        and rows & (rows - 1) == 0
        and planes * rows % 16 == 0
        and width % (planes * LANES) == 0
        and target_basis.shape[0] * devices == width
        and target_basis.shape[0] % 16 == 0
    )


def shards(tokens, expert_ids, gate_codes, gate_weight, up_weight, down_weight, target_basis):
    plan = sharded_basis_shards if fits(tokens, target_basis) else general_shards
    return plan(tokens, expert_ids, gate_codes, gate_weight, up_weight, down_weight, target_basis)


def solution(mesh):
    in_specs = (
        P(("group", "expert"), None),
        P(("group", "expert"), None),
        P(("group", "expert"), None),
        P("expert", None, None),
        P("expert", None, None),
        P("expert", None, None),
        P("expert", None),
    )
    out_specs = P(("group", "expert"), None)
    return jax.shard_map(shards, mesh=mesh, in_specs=in_specs, out_specs=out_specs, check_vma=False)
```

```python
import functools

import jax
import jax.numpy as jnp
from jax import lax
from jax.experimental import pallas as pl
from jax.experimental.pallas import tpu as pltpu
from jax.sharding import PartitionSpec as P


SLICES = 8
CORES = 2
COLUMNS = 2
MAX_PLANES = 4
FETCH_PARTS = 8
LANES = 128
MIB = 1 << 20


def run_expert(received, gate_weight, up_weight, down_weight):
    sources, slots, feature_width = received.shape
    row_block = received.reshape(sources * slots, feature_width)
    gate_act = jnp.dot(row_block, gate_weight[0], preferred_element_type=jnp.float32)
    up_act = jnp.dot(row_block, up_weight[0], preferred_element_type=jnp.float32)
    hidden = (jax.nn.silu(gate_act) * up_act).astype(jnp.bfloat16)
    expert_part = jnp.dot(hidden, down_weight[0], preferred_element_type=jnp.float32).astype(
        jnp.bfloat16
    )
    return expert_part.reshape(sources, slots, feature_width)


def general_shards(
    tokens, expert_ids, gate_codes, gate_weight, up_weight, down_weight, target_basis
):
    token_count, feature_width = tokens.shape
    pick_count = expert_ids.shape[1]
    owner_count = lax.axis_size("expert")
    expert_count = owner_count // SLICES
    capacity = min(token_count, max(2, 5 * token_count * pick_count // (4 * expert_count)))
    rank_width = target_basis.shape[1]
    flat_ids = expert_ids.reshape(-1)
    onehot = (flat_ids[:, None] == jnp.arange(expert_count, dtype=jnp.int32)[None, :]).astype(
        jnp.int32
    )
    before = jnp.cumsum(onehot, axis=0) - onehot
    slot_rank = jnp.sum(before * onehot, axis=1)
    slot_index = flat_ids * capacity + slot_rank
    row_token = jnp.arange(token_count * pick_count, dtype=jnp.int32) // pick_count
    slot_table = (
        jnp.full((expert_count * capacity,), token_count, jnp.int32).at[slot_index].set(row_token)
    )
    padded = jnp.concatenate([tokens, jnp.zeros((1, feature_width), tokens.dtype)], axis=0)
    per_expert_rows = padded[slot_table].reshape(expert_count, 1, capacity, feature_width)
    outgoing = jnp.broadcast_to(per_expert_rows, (expert_count, SLICES, capacity, feature_width))
    outgoing = outgoing.reshape(owner_count, capacity, feature_width)
    full_basis = lax.all_gather(target_basis, "expert", axis=0, tiled=True)
    expert_part = run_expert(
        lax.all_to_all(outgoing, "expert", split_axis=0, concat_axis=0, tiled=True),
        gate_weight,
        up_weight,
        down_weight,
    )
    result = jnp.einsum("skd,dr->skr", expert_part, full_basis, preferred_element_type=jnp.float32)
    returned = lax.all_to_all(result, "expert", split_axis=0, concat_axis=0, tiled=True)
    summed = jnp.sum(returned.reshape(expert_count, SLICES, capacity, rank_width), axis=1)
    projected = summed.reshape(expert_count * capacity, rank_width)[slot_index]
    codes_float = gate_codes.astype(jnp.float32)
    weights = 2.5 * codes_float / jnp.sum(codes_float, axis=1, keepdims=True)
    projected = projected.reshape(token_count, pick_count, rank_width)
    return jnp.sum(weights[:, :, None] * projected, axis=1).astype(jnp.bfloat16)


def fetch_kernel(plan, index_ref, *refs):
    del index_ref
    sources, targets, sems = refs[: -len(plan) - 1], refs[-len(plan) - 1 : -1], refs[-1]
    copies = []
    for (operand, first, count), target in zip(plan, targets):
        rows = target.shape[0] // count
        for k in range(count):
            source = sources[operand].at[pl.ds(first + k * rows, rows), :]
            sem = sems.at[len(copies)]
            copies.append(pltpu.make_async_copy(source, target.at[pl.ds(k * rows, rows), :], sem))
            copies[-1].start()
    for copy in copies:
        copy.wait()


def stack_blocks_kernel(*refs):
    for n, block in enumerate(refs[:-1]):
        refs[-1][n] = block[...]


def stack_rows_kernel(sources, *refs):
    out_ref = refs[-1]
    for n, (ref, at) in enumerate(sources):
        block = refs[ref][...] if at is None else refs[ref][at]
        rows = block.shape[0]
        out_ref[n * rows : (n + 1) * rows, :] = block


def plane_of(index):
    return jnp.right_shift(index, (CORES * COLUMNS).bit_length() - 1)


def place_of(index):
    return jnp.bitwise_and(index, CORES * COLUMNS - 1)


def expert_kernel(order, index_ref, *refs):
    places = CORES * COLUMNS
    stacks = refs[:places]
    gate_ref, up_ref, down_ref = refs[places : places + 3]
    pieces = refs[places + 3 : -1]
    x_ref = refs[-1]
    planes = len(order)
    quarter, width = stacks[0].shape
    rows = quarter // planes
    total = places * quarter
    span = width // planes
    me = plane_of(index_ref[0])
    for b, stack in enumerate(stacks):
        x_ref[b * quarter : (b + 1) * quarter, :] = stack[...]
    x = x_ref[...]
    gate_act = jnp.dot(x, gate_ref[...], preferred_element_type=jnp.float32)
    up_act = jnp.dot(x, up_ref[...], preferred_element_type=jnp.float32)
    hidden = (gate_act / (1.0 + jnp.exp(-gate_act)) * up_act).astype(jnp.bfloat16)
    to_row = lax.broadcasted_iota(jnp.int32, (total, total), 0)
    from_row = lax.broadcasted_iota(jnp.int32, (total, total), 1)
    wanted = jnp.bitwise_xor(from_row, me * rows)
    plane_order = jnp.where(to_row == wanted, 1.0, 0.0).astype(jnp.bfloat16)
    hidden = jnp.dot(plane_order, hidden, preferred_element_type=jnp.float32).astype(jnp.bfloat16)
    for n, step in enumerate(order):
        at = pl.multiple_of(jnp.bitwise_xor(me, step) * span, LANES)
        out = jnp.dot(hidden, down_ref[:, pl.ds(at, span)], preferred_element_type=jnp.float32)
        out = out.astype(jnp.bfloat16)
        for p, piece in enumerate(pieces):
            piece[n] = out[p * quarter : (p + 1) * quarter]


def stack_kernel(shard, index_ref, *refs):
    out_ref = refs[-1]
    place = place_of(index_ref[0])
    taken = 0
    for part in refs[:-1]:
        rows = part.shape[0]
        at = jnp.bitwise_xor(place, taken // shard) * shard + taken % shard
        out_ref[pl.ds(pl.multiple_of(at, 16), rows), :] = part[...]
        taken += rows


def part_total(at, own_ref, other_ref, crossed_ref):
    total = own_ref[at].astype(jnp.float32) + other_ref[at].astype(jnp.float32)
    return total + crossed_ref[at % crossed_ref.shape[0]].astype(jnp.float32)


def total_kernel(at, own_ref, other_ref, crossed_ref, out_ref):
    out_ref[...] = part_total(at, own_ref, other_ref, crossed_ref).astype(out_ref.dtype)


def basis_kernel(per, index_ref, own_ref, other_ref, crossed_ref, *refs):
    planes = (len(refs) - 2) // 2
    parts, basis_ref = refs[: planes - 1], refs[planes - 1]
    outs, s_ref, o_ref = refs[planes:-2], refs[-2], refs[-1]
    quarter = crossed_ref.shape[1]
    experts = planes // per
    rows = quarter // planes
    me = plane_of(index_ref[0])
    for e in range(experts):
        total = part_total(planes - 1, own_ref, other_ref, crossed_ref) if e == 0 else 0.0
        for d in range(max(1, e * per), (e + 1) * per):
            total += parts[d - 1][...].astype(jnp.float32)
        high = total.astype(jnp.bfloat16)
        low = (total - high.astype(jnp.float32)).astype(jnp.bfloat16)
        at = pl.multiple_of(jnp.bitwise_xor(me // per, e) * quarter, quarter)
        s_ref[pl.ds(at, quarter), :] = high
        s_ref[pl.ds(experts * quarter + at, quarter), :] = low
    out = jnp.dot(s_ref[...], basis_ref[...], preferred_element_type=jnp.float32)
    out = out[: experts * quarter] + out[experts * quarter :]
    for e in range(experts):
        for p in range(planes):
            at = e * quarter + p * rows
            o_ref[p, e * rows : (e + 1) * rows, :] = out[at : at + rows]
    for d in range(planes):
        outs[d][...] = o_ref[jnp.bitwise_xor(me, d)]


def sharded_basis_shards(
    tokens, expert_ids, gate_codes, gate_weight, up_weight, down_weight, target_basis
):
    rows, width = tokens.shape
    devices = lax.axis_size("expert")
    place_count = CORES * COLUMNS
    planes = devices // place_count
    experts = devices // SLICES
    quarter = planes * rows
    span = width // planes
    rank = target_basis.shape[1]
    index = lax.axis_index("expert").astype(jnp.int32).reshape(1)
    bf16 = jnp.bfloat16

    def swap(x, step):
        return lax.ppermute(x, "expert", [(i, i ^ step) for i in range(devices)])

    def core_swap(x):
        return swap(x, 1)

    def column_swap(x):
        return swap(x, CORES)

    def plane_swap(x, step):
        return swap(x, place_count * step) if step else x

    vmem = pl.BlockSpec(memory_space=pltpu.VMEM)
    smem = pl.BlockSpec(memory_space=pltpu.SMEM)

    order = sorted(range(planes), key=lambda d: (d < planes // 2, d))
    order = order[: planes // 2] + order[: planes // 2 - 1 : -1]
    near = {d: plane_swap(tokens, d) for d in order}
    own_far = column_swap(tokens)

    hbm = pl.BlockSpec(memory_space=pltpu.HBM)

    def fetch(operands, plan):
        operands = [pltpu.with_memory_space_constraint(x, pltpu.HBM) for x in operands]
        targets = [
            pltpu.VMEM((count, operands[operand].shape[1]), operands[operand].dtype)
            for operand, _, count, _ in plan
        ]
        copies = [(operand, first, count) for operand, first, _, count in plan]
        out = pl.pallas_call(
            functools.partial(fetch_kernel, copies),
            out_shape=tuple(targets),
            in_specs=[smem] + [hbm] * len(operands),
            out_specs=(vmem,) * len(plan),
            scratch_shapes=[pltpu.SemaphoreType.DMA((sum(count for *_, count in plan),))],
            compiler_params=pltpu.CompilerParams(vmem_limit_bytes=MIB),
        )(index, *operands)
        return [pltpu.with_memory_space_constraint(x, pltpu.VMEM) for x in out]

    shard = target_basis.shape[0]
    late = shard // 64 * 16
    gate, up, own, *basis_parts = fetch(
        (gate_weight[0], up_weight[0], tokens, target_basis),
        (
            (0, 0, width, FETCH_PARTS),
            (1, 0, width, FETCH_PARTS),
            (2, 0, rows, 1),
            (3, 0, shard - late, 1),
            (3, shard - late, late, 1),
        ),
    )
    (down,) = fetch((down_weight[0],), ((0, 0, down_weight.shape[1], FETCH_PARTS),))

    def stack(kernel, shape, blocks):
        return pl.pallas_call(
            kernel,
            out_shape=jax.ShapeDtypeStruct(shape, bf16),
            in_specs=[vmem] * len(blocks),
            out_specs=vmem,
            compiler_params=pltpu.CompilerParams(vmem_limit_bytes=4 * MIB),
            name="stack_tokens",
        )(*blocks)

    relayed = stack(
        stack_blocks_kernel, (planes - 1, rows, width), [near[d] for d in range(1, planes)]
    )
    relayed = column_swap(relayed)
    stacks = [
        stack(
            functools.partial(stack_rows_kernel, [(d, None) for d in range(planes)]),
            (quarter, width),
            [own] + [near[d] for d in range(1, planes)],
        ),
        stack(
            functools.partial(
                stack_rows_kernel, [(0, None)] + [(1, d) for d in range(planes - 1)]
            ),
            (quarter, width),
            [own_far, relayed],
        ),
    ]
    stacks += [core_swap(tokens_stack) for tokens_stack in stacks]

    column_parts = [column_swap(x) for x in basis_parts]
    basis_shards = [
        *basis_parts, core_swap(target_basis), *column_parts, *[core_swap(x) for x in column_parts]
    ]

    piece = jax.ShapeDtypeStruct((planes, quarter, span), bf16)
    pieces = pl.pallas_call(
        functools.partial(expert_kernel, order),
        out_shape=(piece,) * place_count,
        in_specs=[smem] + [vmem] * (place_count + 3),
        out_specs=(vmem,) * place_count,
        scratch_shapes=[pltpu.VMEM((place_count * quarter, width), bf16)],
        compiler_params=pltpu.CompilerParams(vmem_limit_bytes=16 * MIB),
        name="expert_work",
    )(index, *stacks, gate, up, down)

    basis = pl.pallas_call(
        functools.partial(stack_kernel, shard),
        out_shape=jax.ShapeDtypeStruct((width // planes, rank), bf16),
        in_specs=[smem] + [vmem] * len(basis_shards),
        out_specs=vmem,
        compiler_params=pltpu.CompilerParams(vmem_limit_bytes=8 * MIB),
        name="stack_basis",
    )(index, *basis_shards)

    own_own, own_far, other_own, other_far = pieces
    other_far = core_swap(other_far)
    other_own = core_swap(other_own)
    pairs = (own_far.astype(jnp.float32) + other_far.astype(jnp.float32)).astype(bf16)
    far_count = planes // 2
    crossed = [column_swap(pairs[:far_count]), column_swap(pairs[far_count:])]
    parts = []
    for d in range(1, planes):
        total = pl.pallas_call(
            functools.partial(total_kernel, order.index(d)),
            out_shape=jax.ShapeDtypeStruct((quarter, span), bf16),
            in_specs=[vmem] * 3,
            out_specs=vmem,
            compiler_params=pltpu.CompilerParams(vmem_limit_bytes=4 * MIB),
        )(own_own, other_own, crossed[d < far_count])
        parts.append(plane_swap(total, d))
    out_piece = jax.ShapeDtypeStruct((experts * rows, rank), jnp.float32)
    partial = pl.pallas_call(
        functools.partial(basis_kernel, SLICES // place_count),
        out_shape=(out_piece,) * planes,
        in_specs=[smem] + [vmem] * (planes + 3),
        out_specs=(vmem,) * planes,
        scratch_shapes=[
            pltpu.VMEM((2 * experts * quarter, span), bf16),
            pltpu.VMEM((planes, experts * rows, rank), jnp.float32),
        ],
        compiler_params=pltpu.CompilerParams(vmem_limit_bytes=16 * MIB),
        name="basis_product",
    )(index, own_own, other_own, crossed[1], *parts, basis)
    projected = sum(plane_swap(partial[d], d) for d in order)
    projected = projected.reshape(experts, rows, rank)
    codes_float = gate_codes.astype(jnp.float32)
    gates = 2.5 * codes_float / jnp.sum(codes_float, axis=1, keepdims=True)
    chosen = expert_ids[None, :, :] == jnp.arange(experts, dtype=jnp.int32)[:, None, None]
    per_expert = jnp.sum(jnp.where(chosen, gates[None, :, :], 0.0), axis=2)
    return jnp.sum(per_expert[:, :, None] * projected, axis=0).astype(bf16)


def fits(tokens, target_basis):
    rows, width = tokens.shape
    devices = lax.axis_size("expert")
    planes = devices // (CORES * COLUMNS)
    return (
        devices % SLICES == 0
        and SLICES % (CORES * COLUMNS) == 0
        and planes & (planes - 1) == 0
        and 1 < planes <= MAX_PLANES
        and rows & (rows - 1) == 0
        and planes * rows % 16 == 0
        and width % (planes * LANES) == 0
        and target_basis.shape[0] * devices == width
        and target_basis.shape[0] % 16 == 0
    )


def shards(tokens, expert_ids, gate_codes, gate_weight, up_weight, down_weight, target_basis):
    plan = sharded_basis_shards if fits(tokens, target_basis) else general_shards
    return plan(tokens, expert_ids, gate_codes, gate_weight, up_weight, down_weight, target_basis)


def solution(mesh):
    in_specs = (
        P(("group", "expert"), None),
        P(("group", "expert"), None),
        P(("group", "expert"), None),
        P("expert", None, None),
        P("expert", None, None),
        P("expert", None, None),
        P("expert", None),
    )
    out_specs = P(("group", "expert"), None)
    return jax.shard_map(shards, mesh=mesh, in_specs=in_specs, out_specs=out_specs, check_vma=False)
```

```python
import functools

import jax
import jax.numpy as jnp
from jax import lax
from jax.experimental import pallas as pl
from jax.experimental.pallas import tpu as pltpu
from jax.sharding import PartitionSpec as P


SLICES = 8
CORES = 2
COLUMNS = 2
PLANES = 4
FETCH_PARTS = 8
LANES = 128
MIB = 1 << 20


def run_expert(received, gate_weight, up_weight, down_weight):
    sources, slots, feature_width = received.shape
    row_block = received.reshape(sources * slots, feature_width)
    gate_act = jnp.dot(row_block, gate_weight[0], preferred_element_type=jnp.float32)
    up_act = jnp.dot(row_block, up_weight[0], preferred_element_type=jnp.float32)
    hidden = (jax.nn.silu(gate_act) * up_act).astype(jnp.bfloat16)
    expert_part = jnp.dot(hidden, down_weight[0], preferred_element_type=jnp.float32).astype(
        jnp.bfloat16
    )
    return expert_part.reshape(sources, slots, feature_width)


def general_shards(
    tokens, expert_ids, gate_codes, gate_weight, up_weight, down_weight, target_basis
):
    token_count, feature_width = tokens.shape
    pick_count = expert_ids.shape[1]
    owner_count = lax.axis_size("expert")
    expert_count = owner_count // SLICES
    capacity = min(token_count, max(2, 5 * token_count * pick_count // (4 * expert_count)))
    rank_width = target_basis.shape[1]
    flat_ids = expert_ids.reshape(-1)
    onehot = (flat_ids[:, None] == jnp.arange(expert_count, dtype=jnp.int32)[None, :]).astype(
        jnp.int32
    )
    before = jnp.cumsum(onehot, axis=0) - onehot
    slot_rank = jnp.sum(before * onehot, axis=1)
    slot_index = flat_ids * capacity + slot_rank
    row_token = jnp.arange(token_count * pick_count, dtype=jnp.int32) // pick_count
    slot_table = (
        jnp.full((expert_count * capacity,), token_count, jnp.int32).at[slot_index].set(row_token)
    )
    padded = jnp.concatenate([tokens, jnp.zeros((1, feature_width), tokens.dtype)], axis=0)
    per_expert_rows = padded[slot_table].reshape(expert_count, 1, capacity, feature_width)
    outgoing = jnp.broadcast_to(per_expert_rows, (expert_count, SLICES, capacity, feature_width))
    outgoing = outgoing.reshape(owner_count, capacity, feature_width)
    full_basis = lax.all_gather(target_basis, "expert", axis=0, tiled=True)
    expert_part = run_expert(
        lax.all_to_all(outgoing, "expert", split_axis=0, concat_axis=0, tiled=True),
        gate_weight,
        up_weight,
        down_weight,
    )
    result = jnp.einsum("skd,dr->skr", expert_part, full_basis, preferred_element_type=jnp.float32)
    returned = lax.all_to_all(result, "expert", split_axis=0, concat_axis=0, tiled=True)
    summed = jnp.sum(returned.reshape(expert_count, SLICES, capacity, rank_width), axis=1)
    projected = summed.reshape(expert_count * capacity, rank_width)[slot_index]
    codes_float = gate_codes.astype(jnp.float32)
    weights = 2.5 * codes_float / jnp.sum(codes_float, axis=1, keepdims=True)
    projected = projected.reshape(token_count, pick_count, rank_width)
    return jnp.sum(weights[:, :, None] * projected, axis=1).astype(jnp.bfloat16)


def fetch_kernel(counts, index_ref, *refs):
    del index_ref
    sources, targets, sems = refs[: len(counts)], refs[len(counts) : -1], refs[-1]
    copies = []
    for source, target, count in zip(sources, targets, counts):
        rows = target.shape[0] // count
        for k in range(count):
            block = pl.ds(k * rows, rows)
            sem = sems.at[len(copies)]
            copies.append(pltpu.make_async_copy(source.at[block, :], target.at[block, :], sem))
            copies[-1].start()
    for copy in copies:
        copy.wait()


def stack_blocks_kernel(*refs):
    for n, block in enumerate(refs[:-1]):
        refs[-1][n] = block[...]


def stack_rows_kernel(sources, *refs):
    out_ref = refs[-1]
    for n, (ref, at) in enumerate(sources):
        block = refs[ref][...] if at is None else refs[ref][at]
        rows = block.shape[0]
        out_ref[n * rows : (n + 1) * rows, :] = block


def bits_of(index):
    return tuple(jnp.bitwise_and(jnp.right_shift(index, n), 1) for n in range(4))


def expert_kernel(index_ref, *refs):
    places = CORES * COLUMNS
    stacks = refs[:places]
    gate_ref, up_ref, down_ref = refs[places : places + 3]
    pieces, x_ref = refs[places + 3 : -1], refs[-1]
    quarter, width = stacks[0].shape
    half = COLUMNS * quarter
    rows = quarter // PLANES
    total = CORES * half
    span = width // (COLUMNS * PLANES)
    _, column, near, far = bits_of(index_ref[0])
    for b, stack in enumerate(stacks):
        x_ref[b * quarter : (b + 1) * quarter, :] = stack[...]
    x = x_ref[...]
    gate_act = jnp.dot(x, gate_ref[...], preferred_element_type=jnp.float32)
    up_act = jnp.dot(x, up_ref[...], preferred_element_type=jnp.float32)
    hidden = (gate_act / (1.0 + jnp.exp(-gate_act)) * up_act).astype(jnp.bfloat16)
    to_row = lax.broadcasted_iota(jnp.int32, (total, total), 0)
    from_row = lax.broadcasted_iota(jnp.int32, (total, total), 1)
    wanted = jnp.bitwise_xor(from_row, column * quarter + (far * 2 + near) * rows)
    order = jnp.where(to_row == wanted, 1.0, 0.0).astype(jnp.bfloat16)
    hidden = jnp.dot(order, hidden, preferred_element_type=jnp.float32).astype(jnp.bfloat16)
    for to_column in (1, 0):
        for n, to_near in enumerate((1, 0)):
            for to_far in (0, 1):
                plane = to_far * 2 + jnp.bitwise_xor(near, to_near)
                chip = plane * COLUMNS + jnp.bitwise_xor(column, to_column)
                part = pl.ds(pl.multiple_of(chip * span, LANES), span)
                out = jnp.dot(hidden, down_ref[:, part], preferred_element_type=jnp.float32)
                out = out.astype(jnp.bfloat16)
                for core in range(CORES):
                    piece = pieces[core * COLUMNS + to_column]
                    at = slice(to_far * span, (to_far + 1) * span)
                    piece[n, :, at] = out[core * half : (core + 1) * half]


def pick_kernel(index_ref, first, second, out_ref):
    group = jnp.right_shift(index_ref[0], 4)
    core = bits_of(index_ref[0])[0]

    @pl.when(core == group)
    def _():
        out_ref[...] = first[...]

    @pl.when(core != group)
    def _():
        out_ref[...] = second[...]


def stack_kernel(index_ref, *refs):
    core, _, _, far = bits_of(index_ref[0])
    place = far * 2 + core
    for b, shard in enumerate(refs[:-1]):
        rows = shard.shape[0]
        at = pl.multiple_of(jnp.bitwise_xor(place, b) * rows, rows)
        refs[-1][pl.ds(at, rows), :] = shard[...]


def part_total(at, own_ref, other_ref, crossed_ref):
    total = own_ref[at].astype(jnp.float32) + other_ref[at].astype(jnp.float32)
    return total + crossed_ref[0].astype(jnp.float32)


def total_kernel(own_ref, other_ref, crossed_ref, out_ref):
    out_ref[...] = part_total(0, own_ref, other_ref, crossed_ref).astype(out_ref.dtype)


def basis_kernel(index_ref, own_ref, other_ref, crossed_ref, near_ref, basis_ref, *refs):
    own_out, other_out, s_ref, o_ref = refs
    half = near_ref.shape[0]
    rows = half // (COLUMNS * PLANES)
    _, column, near, far = bits_of(index_ref[0])
    total = part_total(1, own_ref, other_ref, crossed_ref) + near_ref[...].astype(jnp.float32)
    high = total.astype(jnp.bfloat16)
    s_ref[:half, :] = high
    s_ref[half:, :] = (total - high.astype(jnp.float32)).astype(jnp.bfloat16)
    out = jnp.dot(s_ref[...], basis_ref[...], preferred_element_type=jnp.float32)
    out = out[:half] + out[half:]
    for p in range(COLUMNS * PLANES):
        o_ref[p] = out[p * rows : (p + 1) * rows]
    for n, step in enumerate((0, 2, 1, 3)):
        plane = jnp.bitwise_xor(far * 2 + near, step)
        own_out[n] = o_ref[column * PLANES + plane]
        other_out[n] = o_ref[(1 - column) * PLANES + plane]


def combine_kernel(index_ref, ids_ref, codes_ref, own_ref, far_ref, out_ref):
    expert = bits_of(index_ref[0])[3]
    codes = codes_ref[...].astype(jnp.float32)
    gates = 2.5 * codes / jnp.sum(codes, axis=1, keepdims=True)
    ids = ids_ref[...]
    total = 0.0
    for e, ref in ((expert, own_ref), (1 - expert, far_ref)):
        gate = jnp.sum(jnp.where(ids == e, gates, 0.0), axis=1, keepdims=True)
        total += gate * ref[0]
    out_ref[...] = total.astype(out_ref.dtype)


def sharded_basis_shards(
    tokens, expert_ids, gate_codes, gate_weight, up_weight, down_weight, target_basis
):
    rows, width = tokens.shape
    devices = lax.axis_size("expert")
    place_count = CORES * COLUMNS
    quarter = PLANES * rows
    half = COLUMNS * quarter
    span = 2 * width // (COLUMNS * PLANES)
    shard, rank = target_basis.shape
    index = lax.axis_index(("group", "expert")).astype(jnp.int32).reshape(1)
    bf16 = jnp.bfloat16
    vmem = pl.BlockSpec(memory_space=pltpu.VMEM)
    smem = pl.BlockSpec(memory_space=pltpu.SMEM)
    hbm = pl.BlockSpec(memory_space=pltpu.HBM)

    def swap(x, step):
        return lax.ppermute(x, "expert", [(i, i ^ step) for i in range(devices)])

    def core_swap(x):
        return swap(x, 1)

    def column_swap(x):
        return swap(x, CORES)

    def plane_swap(x, step):
        return swap(x, place_count * step)

    def kernel(body, shapes, *operands, scratch=(), limit=4 * MIB, with_index=True):
        operands = ((index,) if with_index else ()) + operands
        specs = ([smem] if with_index else []) + [vmem] * (len(operands) - with_index)
        return pl.pallas_call(
            body,
            out_shape=shapes,
            in_specs=specs,
            out_specs=jax.tree.map(lambda _: vmem, shapes),
            scratch_shapes=scratch,
            compiler_params=pltpu.CompilerParams(vmem_limit_bytes=limit),
        )(*operands)

    def shape(*dims, dtype=bf16):
        return jax.ShapeDtypeStruct(dims, dtype)

    def fetch(operands):
        operands = [pltpu.with_memory_space_constraint(x, pltpu.HBM) for x in operands]
        counts = [FETCH_PARTS if x.shape[0] % (16 * FETCH_PARTS) == 0 else 1 for x in operands]
        out = pl.pallas_call(
            functools.partial(fetch_kernel, counts),
            out_shape=tuple(pltpu.VMEM(x.shape, x.dtype) for x in operands),
            in_specs=[smem] + [hbm] * len(operands),
            out_specs=(vmem,) * len(operands),
            scratch_shapes=[pltpu.SemaphoreType.DMA((sum(counts),))],
            compiler_params=pltpu.CompilerParams(vmem_limit_bytes=MIB),
        )(index, *operands)
        return [pltpu.with_memory_space_constraint(x, pltpu.VMEM) for x in out]

    near = {d: plane_swap(tokens, d) for d in (2, 3, 1)}
    own_far = column_swap(tokens)
    gate, up, own = fetch((gate_weight[0], up_weight[0], tokens))
    (down,) = fetch((down_weight[0],))
    near = [near[d] for d in range(1, PLANES)]
    relayed = kernel(stack_blocks_kernel, shape(PLANES - 1, rows, width), *near, with_index=False)
    relayed = column_swap(relayed)
    stacks = [
        kernel(
            functools.partial(stack_rows_kernel, [(d, None) for d in range(PLANES)]),
            shape(quarter, width),
            own,
            *near,
            with_index=False,
        ),
        kernel(
            functools.partial(
                stack_rows_kernel, [(0, None)] + [(1, d) for d in range(PLANES - 1)]
            ),
            shape(quarter, width),
            own_far,
            relayed,
            with_index=False,
        ),
    ]
    stacks += [core_swap(tokens_stack) for tokens_stack in stacks]

    senders = [(g, i) for g in range(CORES) for i in range(devices) if i % CORES == g]
    far_basis = lax.ppermute(
        target_basis,
        ("group", "expert"),
        [(g * devices + i, g * devices + (i ^ 2 * place_count)) for g, i in senders],
    )
    group_basis = lax.ppermute(
        far_basis,
        ("group", "expert"),
        [(g * devices + i, (1 - g) * devices + i) for g, i in senders],
    )
    far_basis = kernel(pick_kernel, shape(shard, rank), far_basis, group_basis)
    basis = kernel(
        stack_kernel,
        shape(place_count * shard, rank),
        target_basis,
        core_swap(target_basis),
        far_basis,
        core_swap(far_basis),
    )

    piece = shape(2, half, span)
    own_own, own_far, other_own, other_far = kernel(
        expert_kernel,
        (piece,) * place_count,
        *stacks,
        gate,
        up,
        down,
        scratch=[pltpu.VMEM((place_count * quarter, width), bf16)],
        limit=16 * MIB,
    )

    other_far = core_swap(other_far)
    other_own = core_swap(other_own)
    pairs = (own_far.astype(jnp.float32) + other_far.astype(jnp.float32)).astype(bf16)
    first = column_swap(pairs[:1])
    second = column_swap(pairs[1:])
    total = kernel(total_kernel, shape(half, span), own_own, other_own, first, with_index=False)
    out_piece = shape(PLANES, rows, rank, dtype=jnp.float32)
    kept, sent = kernel(
        basis_kernel,
        (out_piece, out_piece),
        own_own,
        other_own,
        second,
        plane_swap(total, 1),
        basis,
        scratch=[
            pltpu.VMEM((2 * half, span), bf16),
            pltpu.VMEM((COLUMNS * PLANES, rows, rank), jnp.float32),
        ],
        limit=16 * MIB,
    )
    kept = kept + column_swap(sent)
    kept = kept[:2] + plane_swap(kept[2:], 1)
    return kernel(
        combine_kernel, shape(rows, rank), expert_ids, gate_codes, kept[:1], plane_swap(kept[1:], 2)
    )


def fits(tokens, target_basis):
    rows, width = tokens.shape
    devices = lax.axis_size("expert")
    return (
        lax.axis_size("group") == CORES
        and devices == CORES * COLUMNS * PLANES
        and SLICES * 2 == devices
        and rows & (rows - 1) == 0
        and PLANES * rows % 16 == 0
        and width % (COLUMNS * PLANES * LANES) == 0
        and target_basis.shape[0] * devices == width
        and target_basis.shape[0] % 16 == 0
    )


def shards(tokens, expert_ids, gate_codes, gate_weight, up_weight, down_weight, target_basis):
    plan = sharded_basis_shards if fits(tokens, target_basis) else general_shards
    return plan(tokens, expert_ids, gate_codes, gate_weight, up_weight, down_weight, target_basis)


def solution(mesh):
    in_specs = (
        P(("group", "expert"), None),
        P(("group", "expert"), None),
        P(("group", "expert"), None),
        P("expert", None, None),
        P("expert", None, None),
        P("expert", None, None),
        P("expert", None),
    )
    out_specs = P(("group", "expert"), None)
    return jax.shard_map(shards, mesh=mesh, in_specs=in_specs, out_specs=out_specs, check_vma=False)
```

```python
import functools

import jax
import jax.numpy as jnp
from jax import lax
from jax.experimental import pallas as pl
from jax.experimental.pallas import tpu as pltpu
from jax.sharding import PartitionSpec as P


SLICES = 8
CORES = 2
COLUMNS = 2
PLANES = 4
FETCH_PARTS = 8
LANES = 128
MIB = 1 << 20


def run_expert(received, gate_weight, up_weight, down_weight):
    sources, slots, feature_width = received.shape
    row_block = received.reshape(sources * slots, feature_width)
    gate_act = jnp.dot(row_block, gate_weight[0], preferred_element_type=jnp.float32)
    up_act = jnp.dot(row_block, up_weight[0], preferred_element_type=jnp.float32)
    hidden = (jax.nn.silu(gate_act) * up_act).astype(jnp.bfloat16)
    expert_part = jnp.dot(hidden, down_weight[0], preferred_element_type=jnp.float32).astype(
        jnp.bfloat16
    )
    return expert_part.reshape(sources, slots, feature_width)


def general_shards(
    tokens, expert_ids, gate_codes, gate_weight, up_weight, down_weight, target_basis
):
    token_count, feature_width = tokens.shape
    pick_count = expert_ids.shape[1]
    owner_count = lax.axis_size("expert")
    expert_count = owner_count // SLICES
    capacity = min(token_count, max(2, 5 * token_count * pick_count // (4 * expert_count)))
    rank_width = target_basis.shape[1]
    flat_ids = expert_ids.reshape(-1)
    onehot = (flat_ids[:, None] == jnp.arange(expert_count, dtype=jnp.int32)[None, :]).astype(
        jnp.int32
    )
    before = jnp.cumsum(onehot, axis=0) - onehot
    slot_rank = jnp.sum(before * onehot, axis=1)
    slot_index = flat_ids * capacity + slot_rank
    row_token = jnp.arange(token_count * pick_count, dtype=jnp.int32) // pick_count
    slot_table = (
        jnp.full((expert_count * capacity,), token_count, jnp.int32).at[slot_index].set(row_token)
    )
    padded = jnp.concatenate([tokens, jnp.zeros((1, feature_width), tokens.dtype)], axis=0)
    per_expert_rows = padded[slot_table].reshape(expert_count, 1, capacity, feature_width)
    outgoing = jnp.broadcast_to(per_expert_rows, (expert_count, SLICES, capacity, feature_width))
    outgoing = outgoing.reshape(owner_count, capacity, feature_width)
    full_basis = lax.all_gather(target_basis, "expert", axis=0, tiled=True)
    expert_part = run_expert(
        lax.all_to_all(outgoing, "expert", split_axis=0, concat_axis=0, tiled=True),
        gate_weight,
        up_weight,
        down_weight,
    )
    result = jnp.einsum("skd,dr->skr", expert_part, full_basis, preferred_element_type=jnp.float32)
    returned = lax.all_to_all(result, "expert", split_axis=0, concat_axis=0, tiled=True)
    summed = jnp.sum(returned.reshape(expert_count, SLICES, capacity, rank_width), axis=1)
    projected = summed.reshape(expert_count * capacity, rank_width)[slot_index]
    codes_float = gate_codes.astype(jnp.float32)
    weights = 2.5 * codes_float / jnp.sum(codes_float, axis=1, keepdims=True)
    projected = projected.reshape(token_count, pick_count, rank_width)
    return jnp.sum(weights[:, :, None] * projected, axis=1).astype(jnp.bfloat16)


def fetch_kernel(plan, index_ref, *refs):
    sources, targets, sems = refs[: -len(plan) - 1], refs[-len(plan) - 1 : -1], refs[-1]
    group = group_of(index_ref[0])
    copies = []
    for (operand, count), target in zip(plan, targets):
        source = sources[operand]
        rows = target.shape[0] // count
        first = 0 if source.shape[0] == target.shape[0] else group * target.shape[0]
        for k in range(count):
            block = pl.ds(first + k * rows, rows)
            copy = pltpu.make_async_copy(
                source.at[block, :], target.at[pl.ds(k * rows, rows), :], sems.at[len(copies)]
            )
            copy.start()
            copies.append(copy)
    for copy in copies:
        copy.wait()


def stack_blocks_kernel(*refs):
    for n, block in enumerate(refs[:-1]):
        refs[-1][n] = block[...]


def stack_rows_kernel(sources, *refs):
    out_ref = refs[-1]
    for n, (ref, at) in enumerate(sources):
        block = refs[ref][...] if at is None else refs[ref][at]
        rows = block.shape[0]
        out_ref[n * rows : (n + 1) * rows, :] = block


def group_of(index):
    return jnp.right_shift(index, (CORES * COLUMNS * PLANES).bit_length() - 1)


def plane_of(index):
    return jnp.bitwise_and(jnp.right_shift(index, (CORES * COLUMNS).bit_length() - 1), PLANES - 1)


def place_of(index):
    return jnp.bitwise_and(index, CORES * COLUMNS - 1)


def expert_kernel(order, index_ref, *refs):
    places = CORES * COLUMNS
    stacks = refs[:places]
    gate_ref, up_ref, down_ref = refs[places : places + 3]
    pieces = refs[places + 3 : -1]
    x_ref = refs[-1]
    planes = len(order)
    quarter, width = stacks[0].shape
    rows = quarter // planes
    total = places * quarter
    span = width // planes
    me = plane_of(index_ref[0])
    for b, stack in enumerate(stacks):
        x_ref[b * quarter : (b + 1) * quarter, :] = stack[...]
    x = x_ref[...]
    gate_act = jnp.dot(x, gate_ref[...], preferred_element_type=jnp.float32)
    up_act = jnp.dot(x, up_ref[...], preferred_element_type=jnp.float32)
    hidden = (gate_act / (1.0 + jnp.exp(-gate_act)) * up_act).astype(jnp.bfloat16)
    to_row = lax.broadcasted_iota(jnp.int32, (total, total), 0)
    from_row = lax.broadcasted_iota(jnp.int32, (total, total), 1)
    wanted = jnp.bitwise_xor(from_row, me * rows)
    plane_order = jnp.where(to_row == wanted, 1.0, 0.0).astype(jnp.bfloat16)
    hidden = jnp.dot(plane_order, hidden, preferred_element_type=jnp.float32).astype(jnp.bfloat16)
    for n, step in enumerate(order):
        at = pl.multiple_of(jnp.bitwise_xor(me, step) * span, LANES)
        out = jnp.dot(hidden, down_ref[:, pl.ds(at, span)], preferred_element_type=jnp.float32)
        out = out.astype(jnp.bfloat16)
        for p, piece in enumerate(pieces):
            piece[n] = out[p * quarter : (p + 1) * quarter]


def join_kernel(index_ref, own_ref, other_ref, out_ref):
    rows = own_ref.shape[0]
    group = group_of(index_ref[0])
    out_ref[pl.ds(pl.multiple_of(group * rows, rows), rows), :] = own_ref[...]
    out_ref[pl.ds(pl.multiple_of((1 - group) * rows, rows), rows), :] = other_ref[...]


def stack_kernel(index_ref, *refs):
    place = place_of(index_ref[0])
    for b, shard in enumerate(refs[:-1]):
        rows = shard.shape[0]
        at = pl.multiple_of(jnp.bitwise_xor(place, b) * rows, rows)
        refs[-1][pl.ds(at, rows), :] = shard[...]


def part_total(at, own_ref, other_ref, crossed_ref):
    total = own_ref[at].astype(jnp.float32) + other_ref[at].astype(jnp.float32)
    return total + crossed_ref[at % crossed_ref.shape[0]].astype(jnp.float32)


def total_kernel(at, own_ref, other_ref, crossed_ref, out_ref):
    out_ref[...] = part_total(at, own_ref, other_ref, crossed_ref).astype(out_ref.dtype)


def basis_kernel(per, index_ref, own_ref, other_ref, crossed_ref, *refs):
    planes = (len(refs) - 2) // 2
    parts, basis_ref = refs[: planes - 1], refs[planes - 1]
    outs, s_ref, o_ref = refs[planes:-2], refs[-2], refs[-1]
    quarter = crossed_ref.shape[1]
    experts = planes // per
    rows = quarter // planes
    me = plane_of(index_ref[0])
    for e in range(experts):
        total = part_total(planes - 1, own_ref, other_ref, crossed_ref) if e == 0 else 0.0
        for d in range(max(1, e * per), (e + 1) * per):
            total += parts[d - 1][...].astype(jnp.float32)
        high = total.astype(jnp.bfloat16)
        low = (total - high.astype(jnp.float32)).astype(jnp.bfloat16)
        at = pl.multiple_of(jnp.bitwise_xor(me // per, e) * quarter, quarter)
        s_ref[pl.ds(at, quarter), :] = high
        s_ref[pl.ds(experts * quarter + at, quarter), :] = low
    out = jnp.dot(s_ref[...], basis_ref[...], preferred_element_type=jnp.float32)
    out = out[: experts * quarter] + out[experts * quarter :]
    for e in range(experts):
        for p in range(planes):
            at = e * quarter + p * rows
            o_ref[p, e * rows : (e + 1) * rows, :] = out[at : at + rows]
    for d in range(planes):
        outs[d][...] = o_ref[jnp.bitwise_xor(me, d)]


def sharded_basis_shards(
    tokens, expert_ids, gate_codes, gate_weight, up_weight, down_weight, target_basis
):
    rows, width = tokens.shape
    devices = lax.axis_size("expert")
    place_count = CORES * COLUMNS
    planes = devices // place_count
    experts = devices // SLICES
    quarter = planes * rows
    span = width // planes
    rank = target_basis.shape[1]
    index = lax.axis_index(("group", "expert")).astype(jnp.int32).reshape(1)
    bf16 = jnp.bfloat16

    def swap(x, step):
        return lax.ppermute(x, "expert", [(i, i ^ step) for i in range(devices)])

    def core_swap(x):
        return swap(x, 1)

    def column_swap(x):
        return swap(x, CORES)

    def plane_swap(x, step):
        return swap(x, place_count * step) if step else x

    vmem = pl.BlockSpec(memory_space=pltpu.VMEM)
    smem = pl.BlockSpec(memory_space=pltpu.SMEM)

    order = sorted(range(planes), key=lambda d: (d < planes // 2, d))
    order = order[: planes // 2] + order[: planes // 2 - 1 : -1]
    near = {d: plane_swap(tokens, d) for d in order}
    own_far = column_swap(tokens)

    hbm = pl.BlockSpec(memory_space=pltpu.HBM)

    def fetch(operands, plan):
        operands = [pltpu.with_memory_space_constraint(x, pltpu.HBM) for x in operands]
        targets = [
            pltpu.VMEM((count, operands[operand].shape[1]), operands[operand].dtype)
            for operand, count, _ in plan
        ]
        copies = [(operand, count) for operand, _, count in plan]
        out = pl.pallas_call(
            functools.partial(fetch_kernel, copies),
            out_shape=tuple(targets),
            in_specs=[smem] + [hbm] * len(operands),
            out_specs=(vmem,) * len(plan),
            scratch_shapes=[pltpu.SemaphoreType.DMA((sum(count for *_, count in plan),))],
            compiler_params=pltpu.CompilerParams(vmem_limit_bytes=MIB),
        )(index, *operands)
        return [pltpu.with_memory_space_constraint(x, pltpu.VMEM) for x in out]

    shard = target_basis.shape[0]
    gate, up, own, basis_half = fetch(
        (gate_weight[0], up_weight[0], tokens, target_basis),
        (
            (0, width, FETCH_PARTS),
            (1, width, FETCH_PARTS),
            (2, rows, 1),
            (3, shard // 2, 1),
        ),
    )
    (down,) = fetch((down_weight[0],), ((0, down_weight.shape[1], FETCH_PARTS),))

    def stack(kernel, shape, blocks):
        return pl.pallas_call(
            kernel,
            out_shape=jax.ShapeDtypeStruct(shape, bf16),
            in_specs=[vmem] * len(blocks),
            out_specs=vmem,
            compiler_params=pltpu.CompilerParams(vmem_limit_bytes=4 * MIB),
            name="stack_tokens",
        )(*blocks)

    relayed = stack(
        stack_blocks_kernel, (planes - 1, rows, width), [near[d] for d in range(1, planes)]
    )
    relayed = column_swap(relayed)
    stacks = [
        stack(
            functools.partial(stack_rows_kernel, [(d, None) for d in range(planes)]),
            (quarter, width),
            [own] + [near[d] for d in range(1, planes)],
        ),
        stack(
            functools.partial(
                stack_rows_kernel, [(0, None)] + [(1, d) for d in range(planes - 1)]
            ),
            (quarter, width),
            [own_far, relayed],
        ),
    ]
    stacks += [core_swap(tokens_stack) for tokens_stack in stacks]

    column_half = column_swap(basis_half)
    group_half = lax.ppermute(
        column_half,
        ("group", "expert"),
        [(i, (i + devices) % (2 * devices)) for i in range(2 * devices)],
    )
    column_basis = pl.pallas_call(
        join_kernel,
        out_shape=jax.ShapeDtypeStruct((shard, rank), bf16),
        in_specs=[smem, vmem, vmem],
        out_specs=vmem,
        compiler_params=pltpu.CompilerParams(vmem_limit_bytes=4 * MIB),
        name="join_basis",
    )(index, column_half, group_half)
    basis_shards = [target_basis, core_swap(target_basis), column_basis, core_swap(column_basis)]

    piece = jax.ShapeDtypeStruct((planes, quarter, span), bf16)
    pieces = pl.pallas_call(
        functools.partial(expert_kernel, order),
        out_shape=(piece,) * place_count,
        in_specs=[smem] + [vmem] * (place_count + 3),
        out_specs=(vmem,) * place_count,
        scratch_shapes=[pltpu.VMEM((place_count * quarter, width), bf16)],
        compiler_params=pltpu.CompilerParams(vmem_limit_bytes=16 * MIB),
        name="expert_work",
    )(index, *stacks, gate, up, down)

    basis = pl.pallas_call(
        stack_kernel,
        out_shape=jax.ShapeDtypeStruct((width // planes, rank), bf16),
        in_specs=[smem] + [vmem] * len(basis_shards),
        out_specs=vmem,
        compiler_params=pltpu.CompilerParams(vmem_limit_bytes=8 * MIB),
        name="stack_basis",
    )(index, *basis_shards)

    own_own, own_far, other_own, other_far = pieces
    other_far = core_swap(other_far)
    other_own = core_swap(other_own)
    pairs = (own_far.astype(jnp.float32) + other_far.astype(jnp.float32)).astype(bf16)
    far_count = planes // 2
    crossed = [column_swap(pairs[:far_count]), column_swap(pairs[far_count:])]
    parts = []
    for d in range(1, planes):
        total = pl.pallas_call(
            functools.partial(total_kernel, order.index(d)),
            out_shape=jax.ShapeDtypeStruct((quarter, span), bf16),
            in_specs=[vmem] * 3,
            out_specs=vmem,
            compiler_params=pltpu.CompilerParams(vmem_limit_bytes=4 * MIB),
        )(own_own, other_own, crossed[d < far_count])
        parts.append(plane_swap(total, d))
    out_piece = jax.ShapeDtypeStruct((experts * rows, rank), jnp.float32)
    partial = pl.pallas_call(
        functools.partial(basis_kernel, SLICES // place_count),
        out_shape=(out_piece,) * planes,
        in_specs=[smem] + [vmem] * (planes + 3),
        out_specs=(vmem,) * planes,
        scratch_shapes=[
            pltpu.VMEM((2 * experts * quarter, span), bf16),
            pltpu.VMEM((planes, experts * rows, rank), jnp.float32),
        ],
        compiler_params=pltpu.CompilerParams(vmem_limit_bytes=16 * MIB),
        name="basis_product",
    )(index, own_own, other_own, crossed[1], *parts, basis)
    projected = sum(plane_swap(partial[d], d) for d in order)
    projected = projected.reshape(experts, rows, rank)
    codes_float = gate_codes.astype(jnp.float32)
    gates = 2.5 * codes_float / jnp.sum(codes_float, axis=1, keepdims=True)
    chosen = expert_ids[None, :, :] == jnp.arange(experts, dtype=jnp.int32)[:, None, None]
    per_expert = jnp.sum(jnp.where(chosen, gates[None, :, :], 0.0), axis=2)
    return jnp.sum(per_expert[:, :, None] * projected, axis=0).astype(bf16)


def fits(tokens, target_basis):
    rows, width = tokens.shape
    devices = lax.axis_size("expert")
    planes = devices // (CORES * COLUMNS)
    return (
        devices % SLICES == 0
        and SLICES % (CORES * COLUMNS) == 0
        and planes == PLANES
        and lax.axis_size("group") == 2
        and rows & (rows - 1) == 0
        and planes * rows % 16 == 0
        and width % (planes * LANES) == 0
        and target_basis.shape[0] * devices == width
        and target_basis.shape[0] % 32 == 0
    )


def shards(tokens, expert_ids, gate_codes, gate_weight, up_weight, down_weight, target_basis):
    plan = sharded_basis_shards if fits(tokens, target_basis) else general_shards
    return plan(tokens, expert_ids, gate_codes, gate_weight, up_weight, down_weight, target_basis)


def solution(mesh):
    in_specs = (
        P(("group", "expert"), None),
        P(("group", "expert"), None),
        P(("group", "expert"), None),
        P("expert", None, None),
        P("expert", None, None),
        P("expert", None, None),
        P("expert", None),
    )
    out_specs = P(("group", "expert"), None)
    return jax.shard_map(shards, mesh=mesh, in_specs=in_specs, out_specs=out_specs, check_vma=False)
```
